256 devices in a mesh: section: 4 (over y_hi, core), fsdp: 16 (over z, y_lo), batch: 4 (over x).
Axes of the slice: x: 4, y: 4 (y_hi: 2, y_lo: 2; y = y_hi * 2 + y_lo), z: 8, core: 2. Of those that a mesh axis runs over, the one named last changes fastest.
Arguments:
- frames: bfloat16 [4, 64, 48, 1536], P(None, ('fsdp', 'batch')), may hold values from -6 to 6
- cotangent: bfloat16 [4, 64, 48, 1536], P(None, ('fsdp', 'batch')), may hold values from -6 to 6
- lengths: int32 [4, 64], P(None, ('fsdp', 'batch')), may hold values from 24 to 48
- w_in: bfloat16 [4, 1536, 3072], P('section', 'fsdp'), may hold values from -0.15625 to 0.15625
- w_out: bfloat16 [4, 1536, 1536], P('section', 'fsdp'), may hold values from -0.15625 to 0.15625
- gain_pre: float32 [4, 1536], P('section'), may hold values from 0.5 to 1.5
- gain_mid: float32 [4, 1536], P('section'), may hold values from 0.5 to 1.5
- w_depth: float32 [4, 31, 1536], P('section'), may hold values from -2 to 2
Outputs:
- input_grads: bfloat16 [4, 4, 64, 48, 1536], P('section', None, ('fsdp', 'batch'))
- grad_w_in: float32 [4, 1536, 3072], P('section', 'fsdp')
- grad_w_out: float32 [4, 1536, 1536], P('section', 'fsdp')
- grad_gain_pre: float32 [4, 1536], P('section')
- grad_gain_mid: float32 [4, 1536], P('section')
- grad_depth: float32 [4, 31, 1536], P('section')
The draws below stay inside these ranges and needn't reach their ends.
Inputs may be any that keep to these rules, and one draw needn't show every extreme that they name: `lengths`: frames at or after an utterance's length are padding.
All inputs are finite; a program needn't handle non-finite values.
Results may differ from the reference program's by a relative error of at most 0.03.
Values may be sent and summed in bfloat16 or wider, within the bound.
No kernel may reach another device: no remote copies, remote signals or barrier semaphores. Data moves between devices by JAX's collectives and lax.ppermute only.
A program may use at most 128 MiB of HBM per device.

```python
import math
import jax
import jax.numpy as jnp
from jax import lax

D = 1536
K = 31
L = 48
MB = 4
SECTIONS = 4
UTT = 64


def set_ends(drawn, stream_key, low, largest):
    dims = drawn.shape
    index_at = [jax.random.randint(jax.random.fold_in(stream_key, axis), (), 0, dims[axis]) for axis in range(len(dims))]
    drawn = drawn.at[tuple(index_at)].set(low)
    longest = dims.index(max(dims))
    index_at[longest] = (index_at[longest] + 1) % dims[longest]
    return drawn.at[tuple(index_at)].set(largest)


def level_of(rng, extent, pieces, low, high):
    def one(position, parts):
        draws = jax.random.uniform(jax.random.fold_in(jax.random.fold_in(rng, 6), position), (parts,), jnp.float32, low / len(pieces), high / len(pieces))
        return jnp.repeat(jnp.exp(draws), extent[position] // parts).reshape((-1,) + (1,) * (len(extent) - position - 1))

    factor_of = one(*pieces[0])
    for cut in pieces[1:]:
        factor_of = factor_of * one(*cut)
    return factor_of


def scatter_about(rng, dims, deviation, reach, pieces=(), held_as=jnp.bfloat16):
    values = deviation * jax.random.normal(rng, dims, jnp.float32)
    if pieces:
        values = values * level_of(rng, dims, pieces, -0.22, 0.18)
    return jnp.clip(values, -reach, reach).astype(held_as)


def setup_inputs(seed: int = 0) -> dict:
    keys = jax.random.split(jax.random.key(seed), 9)
    return {
        "frames": scatter_about(keys[0], (MB, UTT, L, D), 1.0, 6.0, ((1, 64),)),
        "cotangent": scatter_about(keys[1], (MB, UTT, L, D), 1.0, 6.0, ((1, 64),)),
        "lengths": set_ends(jax.random.randint(keys[2], (MB, UTT), L // 2, L + 1), jax.random.fold_in(keys[2], 1), L // 2, L).astype(jnp.int32),
        "w_in": scatter_about(keys[3], (SECTIONS, D, 2 * D), D ** -0.5, 0.15625, ((0, 4), (1, 16))),
        "w_out": scatter_about(keys[4], (SECTIONS, D, D), D ** -0.5, 0.15625, ((0, 4), (1, 16))),
        "gain_pre": jnp.clip(1.0 + 0.1 * jax.random.normal(keys[5], (SECTIONS, D), jnp.float32), 0.5, 1.5),
        "gain_mid": jnp.clip(1.0 + 0.1 * jax.random.normal(keys[6], (SECTIONS, D), jnp.float32), 0.5, 1.5),
        "w_depth": scatter_about(keys[7], (SECTIONS, K, D), 8 ** -0.5, 2.0, ((0, 4),), jnp.float32),
    }


epsilon = 1e-05

def layer_norm(values):
    mean_value = lax.optimization_barrier(jnp.mean(values, axis=-1, keepdims=True))
    centred = values - mean_value
    inv_scale = lax.rsqrt(lax.optimization_barrier(jnp.mean(centred * centred, axis=-1, keepdims=True)) + epsilon)
    return (centred * inv_scale, inv_scale)

def norm_grad(upstream, normed, inv_scale):
    return (upstream - lax.optimization_barrier(jnp.mean(upstream, axis=-1, keepdims=True)) - normed * lax.optimization_barrier(jnp.mean(upstream * normed, axis=-1, keepdims=True))) * inv_scale

def project(left, right):
    batch_rows, length, inner = left.shape
    flat = jnp.dot(left.reshape(batch_rows * length, inner), right, preferred_element_type=jnp.float32)
    return flat.reshape(batch_rows, length, right.shape[1])

def project_back(left, right):
    batch_rows, length, inner = left.shape
    flat = lax.dot_general(left.reshape(batch_rows * length, inner), right, (((1,), (1,)), ((), ())), preferred_element_type=jnp.float32)
    return flat.reshape(batch_rows, length, right.shape[0])

def depthwise(values, taps):
    kernel = taps.shape[0]
    half = kernel // 2
    length = values.shape[1]
    padded = jnp.pad(values, ((0, 0), (half, half), (0, 0)))
    total = padded[:, 0:length, :] * taps[0]
    for offset in range(1, kernel):
        total = total + padded[:, offset:offset + length, :] * taps[offset]
    return total

def section_forward(frames, w_in, w_out, gain_a, gain_b, taps, padding):
    model_width = frames.shape[-1]
    source = frames.astype(jnp.float32)
    normed_in, inv_in = layer_norm(source)
    projected = (normed_in * gain_a).astype(jnp.bfloat16)
    both = project(projected, w_in)
    glu_value = both[..., :model_width]
    glu_gate = jax.nn.sigmoid(both[..., model_width:])
    gated = glu_value * glu_gate * padding
    conv_out = depthwise(gated, taps)
    normed_mid, inv_mid = layer_norm(conv_out)
    scaled_mid = normed_mid * gain_b
    swished = (scaled_mid * jax.nn.sigmoid(scaled_mid)).astype(jnp.bfloat16)
    result = (source + project(swished, w_out)).astype(jnp.bfloat16)
    return (result, (normed_in, inv_in, projected, glu_value, glu_gate, gated, normed_mid, inv_mid, scaled_mid, swished))

def section_backward(upstream, w_in, w_out, gain_a, gain_b, taps, padding, saved):
    normed_in, inv_in, projected, glu_value, glu_gate, gated, normed_mid, inv_mid, scaled_mid, swished = saved
    kernel = taps.shape[0]
    half = kernel // 2
    length = upstream.shape[1]
    swish_grad = project_back(upstream, w_out)
    sigmoid_mid = jax.nn.sigmoid(scaled_mid)
    scaled_grad = swish_grad * (sigmoid_mid + scaled_mid * sigmoid_mid * (1.0 - sigmoid_mid))
    gain_b_grad = lax.optimization_barrier(jnp.sum(scaled_grad * normed_mid, axis=(0, 1)))
    conv_grad = norm_grad(scaled_grad * gain_b, normed_mid, inv_mid)
    padded_in = jnp.pad(gated, ((0, 0), (half, half), (0, 0)))
    taps_grad = jnp.stack([lax.optimization_barrier(jnp.sum(conv_grad * padded_in[:, offset:offset + length, :], axis=(0, 1))) for offset in range(kernel)])
    padded_grad = jnp.pad(conv_grad, ((0, 0), (half, half), (0, 0)))
    gated_grad = padded_grad[:, 2 * half:2 * half + length, :] * taps[0]
    for offset in range(1, kernel):
        gated_grad = gated_grad + padded_grad[:, 2 * half - offset:2 * half - offset + length, :] * taps[offset]
    gated_grad = gated_grad * padding
    value_grad = gated_grad * glu_gate
    gate_grad = gated_grad * glu_value * glu_gate * (1.0 - glu_gate)
    proj_grad = jnp.concatenate([value_grad, gate_grad], axis=-1).astype(jnp.bfloat16)
    input_side = project_back(proj_grad, w_in)
    gain_a_grad = lax.optimization_barrier(jnp.sum(input_side * normed_in, axis=(0, 1)))
    input_grad = (upstream.astype(jnp.float32) + norm_grad(input_side * gain_a, normed_in, inv_in)).astype(jnp.bfloat16)
    return (input_grad, proj_grad, (gain_a_grad, gain_b_grad, taps_grad))

def by_utterance(values, micro_count, utterances):
    length = values.shape[1]
    last_dim = values.shape[2]
    grouped = values.reshape(micro_count, utterances, length, last_dim).transpose(1, 0, 2, 3)
    return grouped.reshape(utterances, micro_count * length, last_dim)

def device_terms(lefts, rights):

    def accumulate(total, pair):
        term = lax.dot_general(pair[0], pair[1], (((0,), (0,)), ((), ())), preferred_element_type=jnp.float32)
        return (total + lax.optimization_barrier(term.astype(jnp.bfloat16)).astype(jnp.float32), None)
    start = jnp.zeros((lefts.shape[2], rights.shape[2]), jnp.float32)
    total, unused = lax.scan(accumulate, start, (lefts, rights))
    return total

def reference(frames, cotangent, lengths, w_in, w_out, gain_pre, gain_mid, w_depth):
    micro_count, utterances, frames_len, model_width = frames.shape
    section_count = w_in.shape[0]
    batch_rows = micro_count * utterances
    positions = jnp.arange(frames_len, dtype=jnp.int32)
    padding = (positions[None, None, :] < lengths[:, :, None]).astype(jnp.float32).reshape(batch_rows, frames_len, 1)
    scale = 1.0 / math.sqrt(micro_count * utterances * frames_len)
    current = frames.reshape(batch_rows, frames_len, model_width)
    section_inputs = []
    for section_index in range(section_count):
        section_inputs.append(current)
        current, unused = section_forward(current, w_in[section_index], w_out[section_index], gain_pre[section_index], gain_mid[section_index], w_depth[section_index], padding)
    upstream = cotangent.reshape(batch_rows, frames_len, model_width)
    grads_in = [None] * section_count
    grads_proj_in = [None] * section_count
    grads_proj_out = [None] * section_count
    grads_pre = [None] * section_count
    grads_mid = [None] * section_count
    grads_taps = [None] * section_count
    for section_index in reversed(range(section_count)):
        params = (w_in[section_index], w_out[section_index], gain_pre[section_index], gain_mid[section_index], w_depth[section_index])
        unused, saved = section_forward(section_inputs[section_index], params[0], params[1], params[2], params[3], params[4], padding)
        input_grad, proj_grad, minor_grads = section_backward(upstream, params[0], params[1], params[2], params[3], params[4], padding, saved)
        grads_proj_in[section_index] = scale * device_terms(by_utterance(saved[2], micro_count, utterances), by_utterance(proj_grad, micro_count, utterances))
        grads_proj_out[section_index] = scale * device_terms(by_utterance(saved[9], micro_count, utterances), by_utterance(upstream, micro_count, utterances))
        grads_pre[section_index] = scale * minor_grads[0]
        grads_mid[section_index] = scale * minor_grads[1]
        grads_taps[section_index] = scale * minor_grads[2]
        grads_in[section_index] = input_grad.reshape(micro_count, utterances, frames_len, model_width)
        upstream = input_grad
    return (jnp.stack(grads_in), jnp.stack(grads_proj_in), jnp.stack(grads_proj_out), jnp.stack(grads_pre), jnp.stack(grads_mid), jnp.stack(grads_taps))
```

```python
import math

import jax
import jax.numpy as jnp
from jax import lax
from jax.sharding import PartitionSpec as P

epsilon = 1e-05
PAIR = 2


def from_behind(x, axis, by):
    peers = lax.axis_size(axis)
    pairs = [(i, i + by) for i in range(peers) if 0 <= i + by < peers]
    return lax.ppermute(x, axis, pairs)


def rotate(x, axis, by):
    peers = lax.axis_size(axis)
    return lax.ppermute(x, axis, [(i, (i + by) % peers) for i in range(peers)])


def swap_pair(x):
    peers = lax.axis_size("fsdp")
    return lax.ppermute(x, "fsdp", [(i, i ^ 1) for i in range(peers)])


def ring_position():
    index = lax.axis_index("fsdp")
    return index // PAIR, index % PAIR


def pick(stacked, index):
    return lax.dynamic_index_in_dim(stacked, index, 0, keepdims=False)


def gather_rows(shard):
    ring = lax.axis_size("fsdp") // PAIR
    half = ring // 2
    at, side = ring_position()
    other = swap_pair(shard)
    pair = jnp.where(side == 0, jnp.stack([shard, other]), jnp.stack([other, shard]))
    whole = jnp.zeros((ring,) + pair.shape, pair.dtype)

    def put(whole, piece, offset):
        return lax.dynamic_update_slice(whole, piece[None], ((at + offset) % ring, 0, 0, 0))

    whole = put(whole, pair, 0)
    up, down = pair, pair
    for hop in range(1, half):
        up = rotate(up, "fsdp", PAIR)
        down = rotate(down, "fsdp", -PAIR)
        whole = put(put(whole, up, ring - hop), down, hop)
    far_up = rotate(up[0], "fsdp", PAIR)
    far_down = rotate(down[1], "fsdp", -PAIR)
    whole = put(whole, jnp.stack([far_up, far_down]), half)
    return whole.reshape((ring * PAIR,) + shard.shape)


def scatter_rows(terms):
    ring = lax.axis_size("fsdp") // PAIR
    half = ring // 2
    at, side = ring_position()
    pairs = terms.reshape((ring, PAIR) + terms.shape[1:])
    far = pick(pairs, (at + half) % ring)
    up = rotate(far[0], "fsdp", PAIR)
    down = rotate(far[1], "fsdp", -PAIR)
    for hop in range(half - 1, 0, -1):
        mine_up = pick(pairs, (at + hop) % ring).astype(jnp.float32)
        mine_down = pick(pairs, (at + ring - hop) % ring).astype(jnp.float32)
        up = up.astype(jnp.float32)
        down = down.astype(jnp.float32)
        if hop == half - 1:
            up = jnp.stack([mine_up[0] + up, mine_up[1]])
            down = jnp.stack([mine_down[0], mine_down[1] + down])
        else:
            up = mine_up + up
            down = mine_down + down
        up = rotate(up.astype(terms.dtype), "fsdp", PAIR)
        down = rotate(down.astype(terms.dtype), "fsdp", -PAIR)
    total = pick(pairs, at).astype(jnp.float32) + up.astype(jnp.float32) + down.astype(jnp.float32)
    mine = jnp.where(side == 0, total[0], total[1])
    theirs = jnp.where(side == 0, total[1], total[0])
    return mine + swap_pair(theirs.astype(terms.dtype)).astype(jnp.float32)


def batch_copies(x):
    return x, rotate(x, "batch", 1), rotate(x, "batch", 2), rotate(x, "batch", 3)


def sum_batch(x):
    own, left, far, right = (part.astype(jnp.float32) for part in batch_copies(x))
    return (own + far) + (left + right)


def layer_norm(values):
    mean_value = jnp.mean(values, axis=-1, keepdims=True)
    centred = values - mean_value
    inv_scale = lax.rsqrt(jnp.mean(centred * centred, axis=-1, keepdims=True) + epsilon)
    return (centred * inv_scale, inv_scale)


def norm_grad(upstream, normed, inv_scale):
    return (
        upstream
        - jnp.mean(upstream, axis=-1, keepdims=True)
        - normed * jnp.mean(upstream * normed, axis=-1, keepdims=True)
    ) * inv_scale


def rows_by(left, right):
    return jnp.dot(left, right, preferred_element_type=jnp.float32)


def rows_back(left, right):
    return lax.dot_general(
        left, right, (((1,), (1,)), ((), ())), preferred_element_type=jnp.float32
    )


def depthwise(values, taps):
    kernel = taps.shape[0]
    half = kernel // 2
    length = values.shape[1]
    padded = jnp.pad(values, ((0, 0), (half, half), (0, 0)))
    total = padded[:, 0:length, :] * taps[0]
    for offset in range(1, kernel):
        total = total + padded[:, offset : offset + length, :] * taps[offset]
    return total


def section_forward(frames, w_in, w_out, gain_a, gain_b, taps, padding):
    source = frames.astype(jnp.float32)
    normed_in, inv_in = layer_norm(source)
    projected = (normed_in * gain_a).astype(jnp.bfloat16)
    parts = w_in.shape[0]
    both = [rows_by(projected[0], w_in[part])[None] for part in range(parts)]
    glu_value = jnp.concatenate(both[: parts // 2], axis=-1)
    glu_gate = jax.nn.sigmoid(jnp.concatenate(both[parts // 2 :], axis=-1))
    gated = glu_value * glu_gate * padding
    conv_out = depthwise(gated, taps)
    normed_mid, inv_mid = layer_norm(conv_out)
    scaled_mid = normed_mid * gain_b
    swished = (scaled_mid * jax.nn.sigmoid(scaled_mid)).astype(jnp.bfloat16)
    result = (source + rows_by(swished[0], w_out)[None]).astype(jnp.bfloat16)
    return (
        result,
        (
            normed_in,
            inv_in,
            projected,
            glu_value,
            glu_gate,
            gated,
            normed_mid,
            inv_mid,
            scaled_mid,
            swished,
        ),
    )


def section_backward(upstream, w_in, w_out, gain_a, gain_b, taps, padding, saved):
    (
        normed_in,
        inv_in,
        projected,
        glu_value,
        glu_gate,
        gated,
        normed_mid,
        inv_mid,
        scaled_mid,
        swished,
    ) = saved
    kernel = taps.shape[0]
    half = kernel // 2
    length = upstream.shape[1]
    swish_grad = rows_back(upstream[0], w_out)[None]
    sigmoid_mid = jax.nn.sigmoid(scaled_mid)
    scaled_grad = swish_grad * (sigmoid_mid + scaled_mid * sigmoid_mid * (1.0 - sigmoid_mid))
    gain_b_grad = jnp.sum(scaled_grad * normed_mid, axis=(0, 1))
    conv_grad = norm_grad(scaled_grad * gain_b, normed_mid, inv_mid)
    padded_in = jnp.pad(gated, ((0, 0), (half, half), (0, 0)))
    taps_grad = jnp.stack(
        [
            jnp.sum(conv_grad * padded_in[:, offset : offset + length, :], axis=(0, 1))
            for offset in range(kernel)
        ]
    )
    padded_grad = jnp.pad(conv_grad, ((0, 0), (half, half), (0, 0)))
    gated_grad = padded_grad[:, 2 * half : 2 * half + length, :] * taps[0]
    for offset in range(1, kernel):
        gated_grad = (
            gated_grad
            + padded_grad[:, 2 * half - offset : 2 * half - offset + length, :] * taps[offset]
        )
    gated_grad = gated_grad * padding
    value_grad = gated_grad * glu_gate
    gate_grad = gated_grad * glu_value * glu_gate * (1.0 - glu_gate)
    proj_grad = jnp.concatenate([value_grad, gate_grad], axis=-1).astype(jnp.bfloat16)
    parts, unused, width = w_in.shape
    input_side = sum(
        rows_back(proj_grad[0, :, part * width : (part + 1) * width], w_in[part])
        for part in range(parts)
    )[None]
    gain_a_grad = jnp.sum(input_side * normed_in, axis=(0, 1))
    input_grad = (
        upstream.astype(jnp.float32) + norm_grad(input_side * gain_a, normed_in, inv_in)
    ).astype(jnp.bfloat16)
    return (input_grad, proj_grad, (gain_a_grad, gain_b_grad, taps_grad))


def saved_zeros(micro_count, frames_len, model_width):
    wide = (micro_count, 1, frames_len, model_width)
    narrow = (micro_count, 1, frames_len, 1)
    return (
        jnp.zeros(wide, jnp.float32),
        jnp.zeros(narrow, jnp.float32),
        jnp.zeros(wide, jnp.bfloat16),
        jnp.zeros(wide, jnp.float32),
        jnp.zeros(wide, jnp.float32),
        jnp.zeros(wide, jnp.float32),
        jnp.zeros(wide, jnp.float32),
        jnp.zeros(narrow, jnp.float32),
        jnp.zeros(wide, jnp.float32),
        jnp.zeros(wide, jnp.bfloat16),
    )


def put_slot(buffers, values, micro_slot):
    return jax.tree.map(
        lambda buffer, value: lax.dynamic_update_index_in_dim(buffer, value, micro_slot, 0),
        buffers,
        values,
    )


def take_slot(buffers, micro_slot):
    return jax.tree.map(
        lambda buffer: lax.dynamic_index_in_dim(buffer, micro_slot, 0, keepdims=False), buffers
    )


def gather_weights(w_in, w_out):
    quarters = lax.axis_size("batch")
    width = w_in.shape[1] // quarters
    mine = lax.dynamic_slice_in_dim(w_in, lax.axis_index("batch") * width, width, 1)
    mine = gather_rows(mine)
    mine = mine.reshape(-1, width)
    w_in_full = lax.all_gather(mine, "batch", axis=0, tiled=False)
    w_out_full = gather_rows(w_out).reshape(-1, w_out.shape[1])
    return w_in_full, w_out_full


def reduce_weights(term_in, term_out, small, scale):
    quarters, depth, width = term_in.shape
    fsdp = lax.axis_size("fsdp")
    rows = depth // fsdp
    small_rows = -(-small.shape[0] // fsdp)
    small_pad = jnp.pad(small, ((0, small_rows * fsdp - small.shape[0]), (0, 0)))
    extra = jnp.pad(
        small_pad.reshape(fsdp, small_rows, depth).astype(jnp.bfloat16),
        ((0, 0), (0, 16 - small_rows), (0, 0)),
    )
    out_terms = jnp.concatenate([term_out.reshape(fsdp, rows, depth), extra], axis=1)
    in_quarter = lax.psum_scatter(term_in, "batch", scatter_dimension=0, tiled=False)
    out_share = scatter_rows(out_terms)
    out_sum = sum_batch(out_share.astype(jnp.bfloat16))
    grad_out = scale * out_sum[:rows]
    small_sum = gather_rows(scale * out_sum[rows : rows + small_rows])
    small_sum = small_sum.reshape(fsdp * small_rows, depth)[: small.shape[0]]
    in_share = scatter_rows(in_quarter.reshape(fsdp, rows, width)).astype(jnp.bfloat16)
    copies = jnp.stack(batch_copies(in_share))
    here = lax.axis_index("batch")
    grad_in = jnp.concatenate(
        [pick(copies, (here + quarters - part) % quarters) for part in range(quarters)], axis=1
    )
    return scale * grad_in.astype(jnp.float32), grad_out, small_sum


def local(frames, cotangent, lengths, w_in, w_out, gain_pre, gain_mid, w_depth):
    section_count = lax.axis_size("section")
    section_index = lax.axis_index("section")
    micro_count = frames.shape[0]
    frames_len = frames.shape[2]
    model_width = frames.shape[3]
    moments = micro_count + section_count - 1
    scale = 1.0 / math.sqrt(
        micro_count * frames_len * lax.axis_size("fsdp") * lax.axis_size("batch")
    )
    w_in_full, w_out_full = gather_weights(w_in[0], w_out[0])
    gain_a = gain_pre[0]
    gain_b = gain_mid[0]
    taps = w_depth[0]
    positions = jnp.arange(frames_len, dtype=jnp.int32)

    def frame_padding(micro_slot):
        return (positions < lengths[micro_slot, 0]).astype(jnp.float32).reshape(1, frames_len, 1)

    stored = saved_zeros(micro_count, frames_len, model_width)
    blank = jnp.zeros((1, frames_len, model_width), jnp.bfloat16)
    outgoing = blank
    for moment in range(moments):
        if moment > 0:
            incoming = from_behind(outgoing, "section", 1)
        else:
            incoming = blank
        if moment < micro_count:
            section_input = jnp.where(section_index == 0, frames[moment], incoming)
        else:
            section_input = incoming
        micro_index = moment - section_index
        active = (micro_index >= 0) & (micro_index < micro_count)
        micro_slot = jnp.clip(micro_index, 0, micro_count - 1)

        def advance(operands, micro_slot=micro_slot):
            current, buffers = operands
            result, saved = section_forward(
                current, w_in_full, w_out_full, gain_a, gain_b, taps, frame_padding(micro_slot)
            )
            return (result, put_slot(buffers, saved, micro_slot))

        def bypass(operands):
            return (jnp.zeros_like(operands[0]), operands[1])

        outgoing, stored = lax.cond(active, advance, bypass, (section_input, stored))
    row_buffers = (
        jnp.zeros((micro_count, frames_len, model_width), jnp.bfloat16),
        jnp.zeros((micro_count, frames_len, 2 * model_width), jnp.bfloat16),
        jnp.zeros((micro_count, frames_len, model_width), jnp.bfloat16),
        jnp.zeros((micro_count, frames_len, model_width), jnp.bfloat16),
        jnp.zeros((micro_count, frames_len, model_width), jnp.bfloat16),
    )
    small_sums = (
        jnp.zeros((model_width,), jnp.float32),
        jnp.zeros((model_width,), jnp.float32),
        jnp.zeros(taps.shape, jnp.float32),
    )
    returning = blank
    for moment in range(moments):
        if moment > 0:
            incoming = from_behind(returning, "section", -1)
        else:
            incoming = blank
        if moment < micro_count:
            upstream = jnp.where(section_index == section_count - 1, cotangent[moment], incoming)
        else:
            upstream = incoming
        micro_index = moment - (section_count - 1 - section_index)
        active = (micro_index >= 0) & (micro_index < micro_count)
        micro_slot = jnp.clip(micro_index, 0, micro_count - 1)

        def retreat(operands, micro_slot=micro_slot):
            current, buffers, totals = operands
            padding = frame_padding(micro_slot)
            saved = take_slot(stored, micro_slot)
            input_grad, proj_grad, minor_grads = section_backward(
                current, w_in_full, w_out_full, gain_a, gain_b, taps, padding, saved
            )
            row_values = (saved[2][0], proj_grad[0], saved[9][0], current[0], input_grad[0])
            buffers = put_slot(buffers, row_values, micro_slot)
            totals = tuple((total + extra for total, extra in zip(totals, minor_grads)))
            return (input_grad, buffers, totals)

        def hold(operands):
            return (jnp.zeros_like(operands[0]), operands[1], operands[2])

        returning, row_buffers, small_sums = lax.cond(
            active, retreat, hold, (upstream, row_buffers, small_sums)
        )
    total_rows = micro_count * frames_len
    parts, unused, width = w_in_full.shape
    proj_rows = row_buffers[0].reshape(total_rows, model_width)
    grad_rows = row_buffers[1].reshape(total_rows, 2 * model_width)
    swish_rows = row_buffers[2].reshape(total_rows, model_width)
    upstream_rows = row_buffers[3].reshape(total_rows, model_width)

    def term(left, right):
        return lax.dot_general(
            left, right, (((0,), (0,)), ((), ())), preferred_element_type=jnp.float32
        ).astype(jnp.bfloat16)

    term_in = jnp.stack(
        [term(proj_rows, grad_rows[:, part * width : (part + 1) * width]) for part in range(parts)]
    )
    term_out = term(swish_rows, upstream_rows)
    small = jnp.concatenate([small_sums[0][None], small_sums[1][None], small_sums[2]], axis=0)
    grad_in, grad_out, small_total = reduce_weights(term_in, term_out, small, scale)
    input_grads = row_buffers[4].reshape(1, micro_count, 1, frames_len, model_width)
    return (
        input_grads,
        grad_in[None],
        grad_out[None],
        small_total[0:1],
        small_total[1:2],
        small_total[2:][None],
    )


def solution(mesh):
    in_specs = (
        P(None, ("fsdp", "batch"), None, None),
        P(None, ("fsdp", "batch"), None, None),
        P(None, ("fsdp", "batch")),
        P("section", "fsdp", None),
        P("section", "fsdp", None),
        P("section", None),
        P("section", None),
        P("section", None, None),
    )
    out_specs = (
        P("section", None, ("fsdp", "batch"), None, None),
        P("section", "fsdp", None),
        P("section", "fsdp", None),
        P("section", None),
        P("section", None),
        P("section", None, None),
    )
    return jax.shard_map(local, mesh=mesh, in_specs=in_specs, out_specs=out_specs, check_vma=False)
```

```python
import functools
import math

import jax
import jax.numpy as jnp
from jax import lax
from jax.experimental import pallas as pl
from jax.experimental.pallas import tpu as pltpu
from jax.sharding import PartitionSpec as P

epsilon = 1e-05
LANES = 128
SUBLANES = 8
MARGIN = 16
GAIN_A = 32
GAIN_B = 40
PARAM_ROWS = 48
VMEM_LIMIT = 64 * 1024 * 1024 - 64 * 1024
PAIR = 2


def rotate(x, axis, by):
    peers = lax.axis_size(axis)
    return lax.ppermute(x, axis, [(i, (i + by) % peers) for i in range(peers)])


def swap_pair(x):
    peers = lax.axis_size("fsdp")
    return lax.ppermute(x, "fsdp", [(i, i ^ 1) for i in range(peers)])


def ring_position():
    index = lax.axis_index("fsdp")
    return index // PAIR, index % PAIR


def pick(stacked, index):
    return lax.dynamic_index_in_dim(stacked, index, 0, keepdims=False)


def gather_rows(shard):
    ring = lax.axis_size("fsdp") // PAIR
    half = ring // 2
    at, side = ring_position()
    other = swap_pair(shard)
    pair = jnp.where(side == 0, jnp.stack([shard, other]), jnp.stack([other, shard]))
    whole = jnp.zeros((ring,) + pair.shape, pair.dtype)

    def put(whole, piece, offset):
        return lax.dynamic_update_slice(whole, piece[None], ((at + offset) % ring, 0, 0, 0))

    whole = put(whole, pair, 0)
    up, down = pair, pair
    for hop in range(1, half):
        up = rotate(up, "fsdp", PAIR)
        down = rotate(down, "fsdp", -PAIR)
        whole = put(put(whole, up, ring - hop), down, hop)
    far_up = rotate(up[0], "fsdp", PAIR)
    far_down = rotate(down[1], "fsdp", -PAIR)
    whole = put(whole, jnp.stack([far_up, far_down]), half)
    return whole.reshape((ring * PAIR,) + shard.shape)


def scatter_rows(terms):
    ring = lax.axis_size("fsdp") // PAIR
    half = ring // 2
    at, side = ring_position()
    pairs = terms.reshape((ring, PAIR) + terms.shape[1:])
    far = pick(pairs, (at + half) % ring)
    up = rotate(far[0], "fsdp", PAIR)
    down = rotate(far[1], "fsdp", -PAIR)
    for hop in range(half - 1, 0, -1):
        mine_up = pick(pairs, (at + hop) % ring).astype(jnp.float32)
        mine_down = pick(pairs, (at + ring - hop) % ring).astype(jnp.float32)
        up = up.astype(jnp.float32)
        down = down.astype(jnp.float32)
        if hop == half - 1:
            up = jnp.stack([mine_up[0] + up, mine_up[1]])
            down = jnp.stack([mine_down[0], mine_down[1] + down])
        else:
            up = mine_up + up
            down = mine_down + down
        up = rotate(up.astype(terms.dtype), "fsdp", PAIR)
        down = rotate(down.astype(terms.dtype), "fsdp", -PAIR)
    total = pick(pairs, at).astype(jnp.float32) + up.astype(jnp.float32) + down.astype(jnp.float32)
    mine = jnp.where(side == 0, total[0], total[1])
    theirs = jnp.where(side == 0, total[1], total[0])
    return mine + swap_pair(theirs.astype(terms.dtype)).astype(jnp.float32)


def batch_copies(x):
    return x, rotate(x, "batch", 1), rotate(x, "batch", 2), rotate(x, "batch", 3)


def sum_batch(x):
    own, left, far, right = (part.astype(jnp.float32) for part in batch_copies(x))
    return (own + far) + (left + right)


def layer_stats(values):
    mean_value = jnp.mean(values, axis=-1, keepdims=True)
    centred = values - mean_value
    inv_scale = lax.rsqrt(jnp.mean(centred * centred, axis=-1, keepdims=True) + epsilon)
    return centred * inv_scale, inv_scale


def norm_grad(upstream, normed, inv_scale):
    return (
        upstream
        - jnp.mean(upstream, axis=-1, keepdims=True)
        - normed * jnp.mean(upstream * normed, axis=-1, keepdims=True)
    ) * inv_scale


def rows_by(left, right):
    return jnp.dot(left, right, preferred_element_type=jnp.float32)


def rows_back(left, right):
    return lax.dot_general(
        left, right, (((1,), (1,)), ((), ())), preferred_element_type=jnp.float32
    )


def write_shifts(shifts, padded):
    span = shifts.shape[1]
    for by in range(SUBLANES):
        shifts[by] = padded[pl.ds(by, span), :]


def clear_margins(padded, length):
    zeros = jnp.zeros((MARGIN, padded.shape[1]), jnp.float32)
    padded[pl.ds(0, MARGIN), :] = zeros
    padded[pl.ds(MARGIN + length, MARGIN), :] = zeros


def each_lane_block(width, body):
    def step(block, carry):
        body(pl.ds(pl.multiple_of(block * LANES, LANES), LANES))
        return carry

    lax.fori_loop(0, width // LANES, step, 0)


def shifted(shifts, offset, length, lanes):
    start = offset // SUBLANES * SUBLANES
    return shifts[offset % SUBLANES, pl.ds(start, length), lanes]


def forward_kernel(
    info, incoming, frames, w_in, w_out, params, *refs, taps, length, width, aliased
):
    refs = refs[aliased:]
    outgoing, x_all, proj_all, swish_all, value_all, gate_all, mid_all, inv_all = refs[:8]
    (
        x_v, w_in_v, w_out_v, params_v, proj_v, swish_v, value_v, gate_v, mid_v, inv_v,
        padded, shifts, conv_v, out_v, in_sems, out_sems,
    ) = refs[8:]
    slot, active, first, valid = info[0], info[1], info[2], info[3]
    parts = w_in_v.shape[0]
    half = taps // 2

    @pl.when(active == 1)
    def run():
        x_copy = pltpu.make_async_copy(incoming, x_v, in_sems.at[0])
        frame_copy = pltpu.make_async_copy(frames.at[slot], x_v, in_sems.at[0])

        @pl.when(first == 1)
        def from_frames():
            frame_copy.start()

        @pl.when(first == 0)
        def from_neighbour():
            x_copy.start()

        params_copy = pltpu.make_async_copy(params, params_v, in_sems.at[1])
        params_copy.start()
        w_in_copies = [
            pltpu.make_async_copy(w_in.at[part], w_in_v.at[part], in_sems.at[2 + part])
            for part in range(parts)
        ]
        for copy in w_in_copies:
            copy.start()
        w_out_copy = pltpu.make_async_copy(w_out, w_out_v, in_sems.at[2 + parts])
        w_out_copy.start()
        saves = []

        def save(source, target):
            copy = pltpu.make_async_copy(source, target, out_sems.at[len(saves)])
            copy.start()
            saves.append(copy)

        clear_margins(padded, length)
        x_copy.wait()
        params_copy.wait()
        source = x_v[...].astype(jnp.float32)
        save(x_v, x_all.at[slot])
        normed_in, unused = layer_stats(source)
        proj_v[...] = (normed_in * params_v[pl.ds(GAIN_A, 1), :]).astype(jnp.bfloat16)
        save(proj_v, proj_all.at[slot])
        part_width = w_in_v.shape[2]
        for part in range(parts):
            w_in_copies[part].wait()
            out = rows_by(proj_v[...], w_in_v[part])
            place = part % (parts // 2)
            lanes = pl.ds(place * part_width, part_width)
            if part < parts // 2:
                value_v[:, lanes] = out
            else:
                gate_v[:, lanes] = jax.nn.sigmoid(out)
        save(value_v, value_all.at[slot])
        save(gate_v, gate_all.at[slot])
        rows = lax.broadcasted_iota(jnp.int32, (length, width), 0)
        mask = (rows < valid).astype(jnp.float32)
        padded[pl.ds(MARGIN, length), :] = value_v[...] * gate_v[...] * mask
        write_shifts(shifts, padded)

        def convolve(lanes):
            total = jnp.zeros((length, LANES), jnp.float32)
            for tap in range(taps):
                weight = params_v[pl.ds(tap, 1), lanes]
                total = total + shifted(shifts, tap + MARGIN - half, length, lanes) * weight
            conv_v[:, lanes] = total

        each_lane_block(width, convolve)
        normed_mid, inv_mid = layer_stats(conv_v[...])
        mid_v[...] = normed_mid
        inv_v[...] = jnp.broadcast_to(inv_mid, inv_v.shape)
        save(mid_v, mid_all.at[slot])
        save(inv_v, inv_all.at[slot])
        scaled_mid = normed_mid * params_v[pl.ds(GAIN_B, 1), :]
        swish_v[...] = (scaled_mid * jax.nn.sigmoid(scaled_mid)).astype(jnp.bfloat16)
        save(swish_v, swish_all.at[slot])
        w_out_copy.wait()
        source = x_v[...].astype(jnp.float32)
        out_v[...] = (source + rows_by(swish_v[...], w_out_v[...])).astype(jnp.bfloat16)
        save(out_v, outgoing)
        for copy in saves:
            copy.wait()


def backward_kernel(
    info, incoming, cotangent, w_in, w_out, params,
    x_all, value_all, gate_all, mid_all, inv_all, *refs, taps, length, width, aliased
):
    refs = refs[aliased:]
    outgoing, input_all, grad_all, up_all, small_all = refs[:5]
    (
        u_v, w_in_v, w_out_v, params_v, x_v, value_v, gate_v, mid_v, inv_v,
        padded, shifts, padded_grad, shifts_grad, conv_v, grad_v, small_v, out_v,
        in_sems, out_sems,
    ) = refs[5:]
    slot, active, first, valid = info[0], info[1], info[2], info[3]
    parts = w_in_v.shape[0]
    half = taps // 2

    @pl.when(active == 1)
    def run():
        u_copy = pltpu.make_async_copy(incoming, u_v, in_sems.at[0])
        given_copy = pltpu.make_async_copy(cotangent.at[slot], u_v, in_sems.at[0])

        @pl.when(first == 1)
        def from_cotangent():
            given_copy.start()

        @pl.when(first == 0)
        def from_neighbour():
            u_copy.start()

        w_out_copy = pltpu.make_async_copy(w_out, w_out_v, in_sems.at[1])
        w_out_copy.start()
        loads = []
        for number, (source, target) in enumerate((
            (params, params_v),
            (value_all.at[slot], value_v),
            (gate_all.at[slot], gate_v),
            (mid_all.at[slot], mid_v),
            (inv_all.at[slot], inv_v),
            (x_all.at[slot], x_v),
        )):
            copy = pltpu.make_async_copy(source, target, in_sems.at[2 + number])
            copy.start()
            loads.append(copy)
        w_in_copies = [
            pltpu.make_async_copy(w_in.at[part], w_in_v.at[part], in_sems.at[8 + part])
            for part in range(parts)
        ]
        for copy in w_in_copies:
            copy.start()
        saves = []

        def save(source, target):
            copy = pltpu.make_async_copy(source, target, out_sems.at[len(saves)])
            copy.start()
            saves.append(copy)

        clear_margins(padded, length)
        clear_margins(padded_grad, length)
        for copy in loads:
            copy.wait()
        rows = lax.broadcasted_iota(jnp.int32, (length, width), 0)
        mask = (rows < valid).astype(jnp.float32)
        padded[pl.ds(MARGIN, length), :] = value_v[...] * gate_v[...] * mask
        write_shifts(shifts, padded)
        u_copy.wait()
        save(u_v, up_all.at[slot])
        w_out_copy.wait()
        swish_grad = rows_back(u_v[...], w_out_v[...])
        normed_mid = mid_v[...]
        gain_b = params_v[pl.ds(GAIN_B, 1), :]
        scaled_mid = normed_mid * gain_b
        sigmoid_mid = jax.nn.sigmoid(scaled_mid)
        scaled_grad = swish_grad * (
            sigmoid_mid + scaled_mid * sigmoid_mid * (1.0 - sigmoid_mid)
        )
        small_v[pl.ds(GAIN_B, 1), :] = jnp.sum(scaled_grad * normed_mid, axis=0, keepdims=True)
        conv_grad = norm_grad(scaled_grad * gain_b, normed_mid, inv_v[:, :1])
        padded_grad[pl.ds(MARGIN, length), :] = conv_grad
        write_shifts(shifts_grad, padded_grad)

        def convolve(lanes):
            total = jnp.zeros((length, LANES), jnp.float32)
            for tap in range(taps):
                weight = params_v[pl.ds(tap, 1), lanes]
                total = total + shifted(shifts_grad, MARGIN + half - tap, length, lanes) * weight
            conv_v[:, lanes] = total

        each_lane_block(width, convolve)

        def correlate(lanes):
            given = padded_grad[pl.ds(MARGIN, length), lanes]
            for tap in range(taps):
                product = given * shifted(shifts, tap + MARGIN - half, length, lanes)
                small_v[pl.ds(tap, 1), lanes] = jnp.sum(product, axis=0, keepdims=True)

        each_lane_block(width, correlate)
        gated_grad = conv_v[...] * mask
        glu_gate = gate_v[...]
        grad_v[:, :width] = (gated_grad * glu_gate).astype(jnp.bfloat16)
        grad_v[:, width:] = (
            gated_grad * value_v[...] * glu_gate * (1.0 - glu_gate)
        ).astype(jnp.bfloat16)
        save(grad_v, grad_all.at[slot])
        part_width = w_in_v.shape[2]
        input_side = jnp.zeros((length, width), jnp.float32)
        for part in range(parts):
            w_in_copies[part].wait()
            lanes = pl.ds(part * part_width, part_width)
            input_side = input_side + rows_back(grad_v[:, lanes], w_in_v[part])
        normed_in, inv_in = layer_stats(x_v[...].astype(jnp.float32))
        small_v[pl.ds(GAIN_A, 1), :] = jnp.sum(input_side * normed_in, axis=0, keepdims=True)
        save(small_v, small_all.at[slot])
        gain_a = params_v[pl.ds(GAIN_A, 1), :]
        out_v[...] = (
            u_v[...].astype(jnp.float32) + norm_grad(input_side * gain_a, normed_in, inv_in)
        ).astype(jnp.bfloat16)
        save(out_v, outgoing)
        save(out_v, input_all.at[slot])
        for copy in saves:
            copy.wait()


def stage_call(kernel, scratch, info, inputs, out_shapes, buffers, taps, length, width, cost, sems):
    anywhere = pl.BlockSpec(memory_space=pl.ANY)
    aliases = {}
    operands = list(inputs)
    aliased = 0
    if buffers is not None:
        aliased = len(buffers)
        aliases = {1 + len(inputs) + number: 1 + number for number in range(aliased)}
        operands += list(buffers)
    in_sems, out_sems = sems
    return pl.pallas_call(
        functools.partial(kernel, taps=taps, length=length, width=width, aliased=aliased),
        grid_spec=pltpu.PrefetchScalarGridSpec(
            num_scalar_prefetch=1,
            grid=(),
            in_specs=[anywhere] * len(operands),
            out_specs=[anywhere] * len(out_shapes),
            scratch_shapes=list(scratch)
            + [pltpu.SemaphoreType.DMA((in_sems,)), pltpu.SemaphoreType.DMA((out_sems,))],
        ),
        out_shape=out_shapes,
        input_output_aliases=aliases,
        compiler_params=pltpu.CompilerParams(vmem_limit_bytes=VMEM_LIMIT),
        cost_estimate=cost,
    )(info, *operands)


def stage_cost(length, width):
    return pl.CostEstimate(
        flops=6 * length * width * width,
        transcendentals=2 * length * width,
        bytes_accessed=6 * width * width,
    )


def forward_stage(info, incoming, frames, w_in, w_out, params, buffers, taps):
    micro, length, width = frames.shape
    f32, bf16 = jnp.float32, jnp.bfloat16
    shape = jax.ShapeDtypeStruct
    outs = [shape((length, width), bf16)] + [
        shape((micro, length, width), dtype) for dtype in (bf16, bf16, bf16, f32, f32, f32)
    ] + [shape((micro, length, LANES), f32)]
    rows = functools.partial(pltpu.VMEM, (length, width))
    span = length + 2 * MARGIN
    scratch = [
        rows(bf16), pltpu.VMEM(w_in.shape, bf16), pltpu.VMEM(w_out.shape, bf16),
        pltpu.VMEM(params.shape, f32), rows(bf16), rows(bf16), rows(f32), rows(f32), rows(f32),
        pltpu.VMEM((length, LANES), f32), pltpu.VMEM((span, width), f32),
        pltpu.VMEM((SUBLANES, span - SUBLANES, width), f32), rows(f32), rows(bf16),
    ]
    return stage_call(
        forward_kernel, scratch, info, (incoming, frames, w_in, w_out, params), outs, buffers,
        taps, length, width, stage_cost(length, width), (3 + w_in.shape[0], 8),
    )


def backward_stage(info, incoming, cotangent, w_in, w_out, params, saved, buffers, taps):
    micro, length, width = cotangent.shape
    f32, bf16 = jnp.float32, jnp.bfloat16
    shape = jax.ShapeDtypeStruct
    outs = [
        shape((length, width), bf16), shape((micro, length, width), bf16),
        shape((micro, length, 2 * width), bf16), shape((micro, length, width), bf16),
        shape((micro,) + params.shape, f32),
    ]
    rows = functools.partial(pltpu.VMEM, (length, width))
    span = length + 2 * MARGIN
    lifted = pltpu.VMEM((SUBLANES, span - SUBLANES, width), f32)
    scratch = [
        rows(bf16), pltpu.VMEM(w_in.shape, bf16), pltpu.VMEM(w_out.shape, bf16),
        pltpu.VMEM(params.shape, f32), rows(bf16), rows(f32), rows(f32), rows(f32),
        pltpu.VMEM((length, LANES), f32), pltpu.VMEM((span, width), f32), lifted,
        pltpu.VMEM((span, width), f32), lifted, rows(f32),
        pltpu.VMEM((length, 2 * width), bf16), pltpu.VMEM(params.shape, f32), rows(bf16),
    ]
    return stage_call(
        backward_kernel, scratch, info, (incoming, cotangent, w_in, w_out, params) + tuple(saved),
        outs, buffers, taps, length, width, stage_cost(length, width), (8 + w_in.shape[0], 5),
    )


def gather_weights(w_in, w_out):
    quarters = lax.axis_size("batch")
    width = w_in.shape[1] // quarters
    mine = lax.dynamic_slice_in_dim(w_in, lax.axis_index("batch") * width, width, 1)
    mine = gather_rows(mine)
    mine = mine.reshape(-1, width)
    w_in_full = lax.all_gather(mine, "batch", axis=0, tiled=False)
    w_out_full = gather_rows(w_out).reshape(-1, w_out.shape[1])
    return w_in_full, w_out_full


def reduce_weights(term_in, term_out, small, scale):
    quarters, depth, width = term_in.shape
    fsdp = lax.axis_size("fsdp")
    rows = depth // fsdp
    small_rows = -(-small.shape[0] // fsdp)
    small_pad = jnp.pad(small, ((0, small_rows * fsdp - small.shape[0]), (0, 0)))
    extra = jnp.pad(
        small_pad.reshape(fsdp, small_rows, depth).astype(jnp.bfloat16),
        ((0, 0), (0, 16 - small_rows), (0, 0)),
    )
    out_terms = jnp.concatenate([term_out.reshape(fsdp, rows, depth), extra], axis=1)
    in_quarter = lax.psum_scatter(term_in, "batch", scatter_dimension=0, tiled=False)
    out_share = scatter_rows(out_terms)
    out_sum = sum_batch(out_share.astype(jnp.bfloat16))
    grad_out = scale * out_sum[:rows]
    small_sum = gather_rows(scale * out_sum[rows : rows + small_rows])
    small_sum = small_sum.reshape(fsdp * small_rows, depth)[: small.shape[0]]
    in_share = scatter_rows(in_quarter.reshape(fsdp, rows, width)).astype(jnp.bfloat16)
    copies = jnp.stack(batch_copies(in_share))
    here = lax.axis_index("batch")
    grad_in = jnp.concatenate(
        [pick(copies, (here + quarters - part) % quarters) for part in range(quarters)], axis=1
    )
    return scale * grad_in.astype(jnp.float32), grad_out, small_sum


def send_active(x, moment, senders, by):
    pairs = [(s, s + by) for s in senders if 0 <= s + by < lax.axis_size("section")]
    return lax.ppermute(x, "section", pairs)


def local(frames, cotangent, lengths, w_in, w_out, gain_pre, gain_mid, w_depth):
    sections = lax.axis_size("section")
    section_index = lax.axis_index("section")
    micro_count = frames.shape[0]
    frames_len = frames.shape[2]
    model_width = frames.shape[3]
    moments = micro_count + sections - 1
    scale = 1.0 / math.sqrt(
        micro_count * frames_len * lax.axis_size("fsdp") * lax.axis_size("batch")
    )
    w_in_full, w_out_full = gather_weights(w_in[0], w_out[0])
    taps = w_depth.shape[1]
    params = jnp.concatenate(
        [
            w_depth[0],
            jnp.zeros((GAIN_A - taps, model_width), jnp.float32),
            gain_pre,
            jnp.zeros((GAIN_B - GAIN_A - 1, model_width), jnp.float32),
            gain_mid,
            jnp.zeros((PARAM_ROWS - GAIN_B - 1, model_width), jnp.float32),
        ],
        axis=0,
    )
    frame_rows = frames.reshape(micro_count, frames_len, model_width)
    cotangent_rows = cotangent.reshape(micro_count, frames_len, model_width)

    def info_at(moment, place, first):
        micro_index = moment - place
        active = (micro_index >= 0) & (micro_index < micro_count)
        slot = jnp.clip(micro_index, 0, micro_count - 1)
        return jnp.stack(
            [slot, active.astype(jnp.int32), first.astype(jnp.int32), lengths[slot, 0]]
        ).astype(jnp.int32)

    def active_at(moment, flipped):
        places = [p for p in range(sections) if 0 <= moment - p < micro_count]
        return [sections - 1 - p for p in places] if flipped else places

    incoming = jnp.zeros((frames_len, model_width), jnp.bfloat16)
    saved = None
    for moment in range(moments):
        info = info_at(moment, section_index, section_index == 0)
        outgoing, *saved = forward_stage(
            info, incoming, frame_rows, w_in_full, w_out_full, params, saved, taps
        )
        if moment < moments - 1:
            incoming = send_active(outgoing, moment, active_at(moment, False), 1)
    x_all, proj_all, swish_all, value_all, gate_all, mid_all, inv_all = saved
    kept = (x_all, value_all, gate_all, mid_all, inv_all)
    place = sections - 1 - section_index
    grads = None
    for moment in range(moments):
        info = info_at(moment, place, place == 0)
        outgoing, *grads = backward_stage(
            info, incoming, cotangent_rows, w_in_full, w_out_full, params, kept, grads, taps
        )
        if moment < moments - 1:
            incoming = send_active(outgoing, moment, active_at(moment, True), -1)
    input_all, grad_all, up_all, small_all = grads
    total_rows = micro_count * frames_len
    parts, unused, width = w_in_full.shape
    proj_rows = proj_all.reshape(total_rows, model_width)
    grad_rows = grad_all.reshape(total_rows, 2 * model_width)
    swish_rows = swish_all.reshape(total_rows, model_width)
    upstream_rows = up_all.reshape(total_rows, model_width)

    def term(left, right):
        return lax.dot_general(
            left, right, (((0,), (0,)), ((), ())), preferred_element_type=jnp.float32
        ).astype(jnp.bfloat16)

    term_in = jnp.stack(
        [term(proj_rows, grad_rows[:, part * width : (part + 1) * width]) for part in range(parts)]
    )
    term_out = term(swish_rows, upstream_rows)
    small_rows = jnp.sum(small_all, axis=0)
    small = jnp.concatenate(
        [
            small_rows[GAIN_A : GAIN_A + 1],
            small_rows[GAIN_B : GAIN_B + 1],
            small_rows[:taps],
        ],
        axis=0,
    )
    grad_in, grad_out, small_total = reduce_weights(term_in, term_out, small, scale)
    input_grads = input_all.reshape(1, micro_count, 1, frames_len, model_width)
    return (
        input_grads,
        grad_in[None],
        grad_out[None],
        small_total[0:1],
        small_total[1:2],
        small_total[2:][None],
    )


def solution(mesh):
    in_specs = (
        P(None, ("fsdp", "batch"), None, None),
        P(None, ("fsdp", "batch"), None, None),
        P(None, ("fsdp", "batch")),
        P("section", "fsdp", None),
        P("section", "fsdp", None),
        P("section", None),
        P("section", None),
        P("section", None, None),
    )
    out_specs = (
        P("section", None, ("fsdp", "batch"), None, None),
        P("section", "fsdp", None),
        P("section", "fsdp", None),
        P("section", None),
        P("section", None),
        P("section", None, None),
    )
    return jax.shard_map(local, mesh=mesh, in_specs=in_specs, out_specs=out_specs, check_vma=False)
```

```python
import functools
import math

import jax
import jax.numpy as jnp
from jax import lax
from jax.experimental import pallas as pl
from jax.experimental.pallas import tpu as pltpu
from jax.sharding import PartitionSpec as P

epsilon = 1e-05
LANES = 128
SUBLANES = 8
MARGIN = 16
GAIN_A = 32
GAIN_B = 40
PARAM_ROWS = 48
SKEW = 2
VMEM_LIMIT = 64 * 1024 * 1024 - 64 * 1024
PAIR = 2


def rotate(x, axis, by):
    peers = lax.axis_size(axis)
    return lax.ppermute(x, axis, [(i, (i + by) % peers) for i in range(peers)])


def swap_pair(x):
    peers = lax.axis_size("fsdp")
    return lax.ppermute(x, "fsdp", [(i, i ^ 1) for i in range(peers)])


def ring_position():
    index = lax.axis_index("fsdp")
    return index // PAIR, index % PAIR


def pick(stacked, index):
    return lax.dynamic_index_in_dim(stacked, index, 0, keepdims=False)


def gather_rows(shard):
    ring = lax.axis_size("fsdp") // PAIR
    half = ring // 2
    at, side = ring_position()
    other = swap_pair(shard)
    pair = jnp.where(side == 0, jnp.stack([shard, other]), jnp.stack([other, shard]))
    whole = jnp.zeros((ring,) + pair.shape, pair.dtype)

    def put(whole, piece, offset):
        return lax.dynamic_update_slice(whole, piece[None], ((at + offset) % ring, 0, 0, 0))

    whole = put(whole, pair, 0)
    up, down = pair, pair
    for hop in range(1, half):
        up = rotate(up, "fsdp", PAIR)
        down = rotate(down, "fsdp", -PAIR)
        whole = put(put(whole, up, ring - hop), down, hop)
    far_up = rotate(up[0], "fsdp", PAIR)
    far_down = rotate(down[1], "fsdp", -PAIR)
    whole = put(whole, jnp.stack([far_up, far_down]), half)
    return whole.reshape((ring * PAIR,) + shard.shape)


def scatter_rows(terms):
    ring = lax.axis_size("fsdp") // PAIR
    half = ring // 2
    at, side = ring_position()
    pairs = terms.reshape((ring, PAIR) + terms.shape[1:])
    far = pick(pairs, (at + half) % ring)
    up = rotate(far[0], "fsdp", PAIR)
    down = rotate(far[1], "fsdp", -PAIR)
    for hop in range(half - 1, 0, -1):
        mine_up = pick(pairs, (at + hop) % ring).astype(jnp.float32)
        mine_down = pick(pairs, (at + ring - hop) % ring).astype(jnp.float32)
        up = up.astype(jnp.float32)
        down = down.astype(jnp.float32)
        if hop == half - 1:
            up = jnp.stack([mine_up[0] + up, mine_up[1]])
            down = jnp.stack([mine_down[0], mine_down[1] + down])
        else:
            up = mine_up + up
            down = mine_down + down
        up = rotate(up.astype(terms.dtype), "fsdp", PAIR)
        down = rotate(down.astype(terms.dtype), "fsdp", -PAIR)
    total = pick(pairs, at).astype(jnp.float32) + up.astype(jnp.float32) + down.astype(jnp.float32)
    mine = jnp.where(side == 0, total[0], total[1])
    theirs = jnp.where(side == 0, total[1], total[0])
    return mine + swap_pair(theirs.astype(terms.dtype)).astype(jnp.float32)


def batch_copies(x):
    return x, rotate(x, "batch", 1), rotate(x, "batch", 2), rotate(x, "batch", 3)


def sum_batch(x):
    own, left, far, right = (part.astype(jnp.float32) for part in batch_copies(x))
    return (own + far) + (left + right)


def layer_stats(values):
    mean_value = jnp.mean(values, axis=-1, keepdims=True)
    centred = values - mean_value
    inv_scale = lax.rsqrt(jnp.mean(centred * centred, axis=-1, keepdims=True) + epsilon)
    return centred * inv_scale, inv_scale


def norm_grad(upstream, normed, inv_scale):
    return (
        upstream
        - jnp.mean(upstream, axis=-1, keepdims=True)
        - normed * jnp.mean(upstream * normed, axis=-1, keepdims=True)
    ) * inv_scale


def rows_by(left, right):
    return jnp.dot(left, right, preferred_element_type=jnp.float32)


def rows_back(left, right):
    return lax.dot_general(
        left, right, (((1,), (1,)), ((), ())), preferred_element_type=jnp.float32
    )


def write_shifts(shifts, padded):
    span = shifts.shape[1]

    def shift(lanes):
        for by in range(SUBLANES):
            shifts[by, :, lanes] = padded[pl.ds(by, span), lanes]

    each_lane_block(padded.shape[1], shift)


def clear_margins(padded, length):
    zeros = jnp.zeros((MARGIN, padded.shape[1]), jnp.float32)
    padded[pl.ds(0, MARGIN), :] = zeros
    padded[pl.ds(MARGIN + length, MARGIN), :] = zeros


def each_block(width, size, body):
    def step(block, carry):
        body(block, pl.ds(pl.multiple_of(block * size, size), size))
        return carry

    lax.fori_loop(0, width // size, step, 0)


def each_lane_block(width, body):
    each_block(width, LANES, lambda block, lanes: body(lanes))


def shifted(shifts, offset, length, lanes):
    start = offset // SUBLANES * SUBLANES
    return shifts[offset % SUBLANES, pl.ds(start, length), lanes]


def forward_kernel(
    info, incoming, frames, w_in, w_out, params, *refs, taps, length, width, aliased
):
    refs = refs[aliased:]
    outgoing, x_all, proj_all, swish_all, value_all, gate_all, mid_all, inv_all = refs[:8]
    (
        x_v, w_in_v, w_out_v, params_v, proj_v, swish_v, value_v, gate_v, mid_v, inv_v,
        padded, shifts, conv_v, out_v, in_sems, out_sems,
    ) = refs[8:]
    slot, active, first, valid = info[0], info[1], info[2], info[3]
    parts = w_in_v.shape[0]
    half = taps // 2

    @pl.when(active == 1)
    def run():
        x_copy = pltpu.make_async_copy(incoming, x_v, in_sems.at[0])
        frame_copy = pltpu.make_async_copy(frames.at[slot], x_v, in_sems.at[0])

        @pl.when(first == 1)
        def from_frames():
            frame_copy.start()

        @pl.when(first == 0)
        def from_neighbour():
            x_copy.start()

        params_copy = pltpu.make_async_copy(params, params_v, in_sems.at[1])
        params_copy.start()
        w_in_copies = [
            pltpu.make_async_copy(w_in.at[part], w_in_v.at[part], in_sems.at[2 + part])
            for part in range(parts)
        ]
        for copy in w_in_copies:
            copy.start()
        w_out_copy = pltpu.make_async_copy(w_out, w_out_v, in_sems.at[2 + parts])
        w_out_copy.start()
        saves = []

        def save(source, target):
            copy = pltpu.make_async_copy(source, target, out_sems.at[len(saves)])
            copy.start()
            saves.append(copy)

        clear_margins(padded, length)
        x_copy.wait()
        params_copy.wait()
        source = x_v[...].astype(jnp.float32)
        save(x_v, x_all.at[slot])
        normed_in, unused = layer_stats(source)
        proj_v[...] = (normed_in * params_v[pl.ds(GAIN_A, 1), :]).astype(jnp.bfloat16)
        save(proj_v, proj_all.at[slot])
        part_width = w_in_v.shape[2]

        def into_value(part, lanes):
            pltpu.make_async_copy(w_in.at[part], w_in_v.at[part], in_sems.at[2 + part]).wait()
            value_v[:, lanes] = rows_by(proj_v[...], w_in_v[part])

        def into_gate(block, lanes):
            part = block + parts // 2
            pltpu.make_async_copy(w_in.at[part], w_in_v.at[part], in_sems.at[2 + part]).wait()
            gate_v[:, lanes] = jax.nn.sigmoid(rows_by(proj_v[...], w_in_v[part]))

        each_block(width, part_width, into_value)
        each_block(width, part_width, into_gate)
        save(value_v, value_all.at[slot])
        save(gate_v, gate_all.at[slot])
        rows = lax.broadcasted_iota(jnp.int32, (length, width), 0)
        mask = (rows < valid).astype(jnp.float32)
        padded[pl.ds(MARGIN, length), :] = value_v[...] * gate_v[...] * mask
        write_shifts(shifts, padded)

        def convolve(lanes):
            total = jnp.zeros((length, LANES), jnp.float32)
            for tap in range(taps):
                weight = params_v[pl.ds(tap, 1), lanes]
                total = total + shifted(shifts, tap + MARGIN - half, length, lanes) * weight
            conv_v[:, lanes] = total

        each_lane_block(width, convolve)
        normed_mid, inv_mid = layer_stats(conv_v[...])
        mid_v[...] = normed_mid
        inv_v[...] = jnp.broadcast_to(inv_mid, inv_v.shape)
        save(mid_v, mid_all.at[slot])
        save(inv_v, inv_all.at[slot])
        scaled_mid = normed_mid * params_v[pl.ds(GAIN_B, 1), :]
        swish_v[...] = (scaled_mid * jax.nn.sigmoid(scaled_mid)).astype(jnp.bfloat16)
        save(swish_v, swish_all.at[slot])
        w_out_copy.wait()

        def into_out(block, lanes):
            source = x_v[:, lanes].astype(jnp.float32)
            out_v[:, lanes] = (source + rows_by(swish_v[...], w_out_v[:, lanes])).astype(
                jnp.bfloat16
            )

        each_block(width, part_width, into_out)
        save(out_v, outgoing)
        for copy in saves:
            copy.wait()


def backward_kernel(
    info, incoming, cotangent, w_in, w_out, params,
    x_all, value_all, gate_all, mid_all, inv_all, *refs, taps, length, width, aliased
):
    refs = refs[aliased:]
    outgoing, input_all, grad_all, up_all, small_all = refs[:5]
    (
        u_v, w_in_v, w_out_v, params_v, x_v, value_v, gate_v, mid_v, inv_v,
        padded, shifts, padded_grad, shifts_grad, conv_v, grad_v, small_v, out_v,
        in_sems, out_sems,
    ) = refs[5:]
    slot, active, first, valid = info[0], info[1], info[2], info[3]
    parts = w_in_v.shape[0]
    half = taps // 2

    @pl.when(active == 1)
    def run():
        u_copy = pltpu.make_async_copy(incoming, u_v, in_sems.at[0])
        given_copy = pltpu.make_async_copy(cotangent.at[slot], u_v, in_sems.at[0])

        @pl.when(first == 1)
        def from_cotangent():
            given_copy.start()

        @pl.when(first == 0)
        def from_neighbour():
            u_copy.start()

        w_out_copy = pltpu.make_async_copy(w_out, w_out_v, in_sems.at[1])
        w_out_copy.start()
        loads = []
        for number, (source, target) in enumerate((
            (params, params_v),
            (value_all.at[slot], value_v),
            (gate_all.at[slot], gate_v),
            (mid_all.at[slot], mid_v),
            (inv_all.at[slot], inv_v),
            (x_all.at[slot], x_v),
        )):
            copy = pltpu.make_async_copy(source, target, in_sems.at[2 + number])
            copy.start()
            loads.append(copy)
        w_in_copies = [
            pltpu.make_async_copy(w_in.at[part], w_in_v.at[part], in_sems.at[8 + part])
            for part in range(parts)
        ]
        for copy in w_in_copies:
            copy.start()
        saves = []

        def save(source, target):
            copy = pltpu.make_async_copy(source, target, out_sems.at[len(saves)])
            copy.start()
            saves.append(copy)

        clear_margins(padded, length)
        clear_margins(padded_grad, length)
        for copy in loads:
            copy.wait()
        rows = lax.broadcasted_iota(jnp.int32, (length, width), 0)
        mask = (rows < valid).astype(jnp.float32)
        padded[pl.ds(MARGIN, length), :] = value_v[...] * gate_v[...] * mask
        write_shifts(shifts, padded)
        u_copy.wait()
        save(u_v, up_all.at[slot])
        w_out_copy.wait()
        part_width = w_in_v.shape[2]

        def into_swish(block, lanes):
            conv_v[:, lanes] = rows_back(u_v[...], w_out_v[lanes, :])

        each_block(width, part_width, into_swish)
        swish_grad = conv_v[...]
        normed_mid = mid_v[...]
        gain_b = params_v[pl.ds(GAIN_B, 1), :]
        scaled_mid = normed_mid * gain_b
        sigmoid_mid = jax.nn.sigmoid(scaled_mid)
        scaled_grad = swish_grad * (
            sigmoid_mid + scaled_mid * sigmoid_mid * (1.0 - sigmoid_mid)
        )
        small_v[pl.ds(GAIN_B, 1), :] = jnp.sum(scaled_grad * normed_mid, axis=0, keepdims=True)
        conv_grad = norm_grad(scaled_grad * gain_b, normed_mid, inv_v[:, :1])
        padded_grad[pl.ds(MARGIN, length), :] = conv_grad
        write_shifts(shifts_grad, padded_grad)

        def convolve(lanes):
            total = jnp.zeros((length, LANES), jnp.float32)
            for tap in range(taps):
                weight = params_v[pl.ds(tap, 1), lanes]
                total = total + shifted(shifts_grad, MARGIN + half - tap, length, lanes) * weight
            conv_v[:, lanes] = total

        each_lane_block(width, convolve)

        def correlate(lanes):
            given = padded_grad[pl.ds(MARGIN, length), lanes]
            for tap in range(taps):
                product = given * shifted(shifts, tap + MARGIN - half, length, lanes)
                small_v[pl.ds(tap, 1), lanes] = jnp.sum(product, axis=0, keepdims=True)

        each_lane_block(width, correlate)
        gated_grad = conv_v[...] * mask
        glu_gate = gate_v[...]
        grad_v[:, :width] = (gated_grad * glu_gate).astype(jnp.bfloat16)
        grad_v[:, width:] = (
            gated_grad * value_v[...] * glu_gate * (1.0 - glu_gate)
        ).astype(jnp.bfloat16)
        save(grad_v, grad_all.at[slot])
        conv_v[...] = jnp.zeros_like(conv_v)

        def into_input(part, lanes):
            pltpu.make_async_copy(w_in.at[part], w_in_v.at[part], in_sems.at[8 + part]).wait()
            conv_v[...] += rows_back(grad_v[:, lanes], w_in_v[part])

        each_block(2 * width, part_width, into_input)
        input_side = conv_v[...]
        normed_in, inv_in = layer_stats(x_v[...].astype(jnp.float32))
        small_v[pl.ds(GAIN_A, 1), :] = jnp.sum(input_side * normed_in, axis=0, keepdims=True)
        save(small_v, small_all.at[slot])
        gain_a = params_v[pl.ds(GAIN_A, 1), :]
        out_v[...] = (
            u_v[...].astype(jnp.float32) + norm_grad(input_side * gain_a, normed_in, inv_in)
        ).astype(jnp.bfloat16)
        save(out_v, outgoing)
        save(out_v, input_all.at[slot])
        for copy in saves:
            copy.wait()


def stage_call(kernel, scratch, info, inputs, out_shapes, buffers, taps, length, width, cost, sems):
    anywhere = pl.BlockSpec(memory_space=pl.ANY)
    aliases = {}
    operands = list(inputs)
    aliased = 0
    if buffers is not None:
        aliased = len(buffers)
        aliases = {1 + len(inputs) + number: 1 + number for number in range(aliased)}
        operands += list(buffers)
    in_sems, out_sems = sems
    return pl.pallas_call(
        functools.partial(kernel, taps=taps, length=length, width=width, aliased=aliased),
        grid_spec=pltpu.PrefetchScalarGridSpec(
            num_scalar_prefetch=1,
            grid=(),
            in_specs=[anywhere] * len(operands),
            out_specs=[anywhere] * len(out_shapes),
            scratch_shapes=list(scratch)
            + [pltpu.SemaphoreType.DMA((in_sems,)), pltpu.SemaphoreType.DMA((out_sems,))],
        ),
        out_shape=out_shapes,
        input_output_aliases=aliases,
        compiler_params=pltpu.CompilerParams(vmem_limit_bytes=VMEM_LIMIT),
        cost_estimate=cost,
    )(info, *operands)


def stage_cost(length, width):
    return pl.CostEstimate(
        flops=6 * length * width * width,
        transcendentals=2 * length * width,
        bytes_accessed=6 * width * width,
    )


def forward_stage(info, incoming, frames, w_in, w_out, params, buffers, taps):
    micro, length, width = frames.shape
    f32, bf16 = jnp.float32, jnp.bfloat16
    shape = jax.ShapeDtypeStruct
    outs = [shape((length, width), bf16)] + [
        shape((micro, length, width), dtype) for dtype in (bf16, bf16, bf16, f32, f32, f32)
    ] + [shape((micro, length, LANES), f32)]
    rows = functools.partial(pltpu.VMEM, (length, width))
    span = length + 2 * MARGIN
    scratch = [
        rows(bf16), pltpu.VMEM(w_in.shape, bf16), pltpu.VMEM(w_out.shape, bf16),
        pltpu.VMEM(params.shape, f32), rows(bf16), rows(bf16), rows(f32), rows(f32), rows(f32),
        pltpu.VMEM((length, LANES), f32), pltpu.VMEM((span, width), f32),
        pltpu.VMEM((SUBLANES, span - SUBLANES, width), f32), rows(f32), rows(bf16),
    ]
    return stage_call(
        forward_kernel, scratch, info, (incoming, frames, w_in, w_out, params), outs, buffers,
        taps, length, width, stage_cost(length, width), (3 + w_in.shape[0], 8),
    )


def backward_stage(info, incoming, cotangent, w_in, w_out, params, saved, buffers, taps):
    micro, length, width = cotangent.shape
    f32, bf16 = jnp.float32, jnp.bfloat16
    shape = jax.ShapeDtypeStruct
    outs = [
        shape((length, width), bf16), shape((micro, length, width), bf16),
        shape((micro, length, 2 * width), bf16), shape((micro, length, width), bf16),
        shape((micro,) + params.shape, f32),
    ]
    rows = functools.partial(pltpu.VMEM, (length, width))
    span = length + 2 * MARGIN
    lifted = pltpu.VMEM((SUBLANES, span - SUBLANES, width), f32)
    scratch = [
        rows(bf16), pltpu.VMEM(w_in.shape, bf16), pltpu.VMEM(w_out.shape, bf16),
        pltpu.VMEM(params.shape, f32), rows(bf16), rows(f32), rows(f32), rows(f32),
        pltpu.VMEM((length, LANES), f32), pltpu.VMEM((span, width), f32), lifted,
        pltpu.VMEM((span, width), f32), lifted, rows(f32),
        pltpu.VMEM((length, 2 * width), bf16), pltpu.VMEM(params.shape, f32), rows(bf16),
    ]
    return stage_call(
        backward_kernel, scratch, info, (incoming, cotangent, w_in, w_out, params) + tuple(saved),
        outs, buffers, taps, length, width, stage_cost(length, width), (8 + w_in.shape[0], 5),
    )


def gather_weights(w_in, w_out):
    quarters = lax.axis_size("batch")
    width = w_in.shape[1] // quarters
    mine = lax.dynamic_slice_in_dim(w_in, lax.axis_index("batch") * width, width, 1)
    mine = gather_rows(mine)
    mine = mine.reshape(-1, width)
    w_in_full = lax.all_gather(mine, "batch", axis=0, tiled=False)
    w_out_full = gather_rows(w_out).reshape(-1, w_out.shape[1])
    return w_in_full, w_out_full


def reduce_weights(term_in, term_out, small, scale):
    quarters, depth, width = term_in.shape
    fsdp = lax.axis_size("fsdp")
    rows = depth // fsdp
    small_rows = -(-small.shape[0] // fsdp)
    small_pad = jnp.pad(small, ((0, small_rows * fsdp - small.shape[0]), (0, 0)))
    extra = jnp.pad(
        small_pad.reshape(fsdp, small_rows, depth).astype(jnp.bfloat16),
        ((0, 0), (0, 16 - small_rows), (0, 0)),
    )
    out_terms = jnp.concatenate([term_out.reshape(fsdp, rows, depth), extra], axis=1)
    in_quarter = lax.psum_scatter(term_in, "batch", scatter_dimension=0, tiled=False)
    out_share = scatter_rows(out_terms)
    out_sum = sum_batch(out_share.astype(jnp.bfloat16))
    grad_out = scale * out_sum[:rows]
    small_sum = gather_rows(scale * out_sum[rows : rows + small_rows])
    small_sum = small_sum.reshape(fsdp * small_rows, depth)[: small.shape[0]]
    in_share = scatter_rows(in_quarter.reshape(fsdp, rows, width)).astype(jnp.bfloat16)
    copies = jnp.stack(batch_copies(in_share))
    here = lax.axis_index("batch")
    grad_in = jnp.concatenate(
        [pick(copies, (here + quarters - part) % quarters) for part in range(quarters)], axis=1
    )
    return scale * grad_in.astype(jnp.float32), grad_out, small_sum


def send_active(x, senders, by):
    pairs = [(s, s + by) for s in senders if 0 <= s + by < lax.axis_size("section")]
    return lax.ppermute(x, "section", pairs)


def local(frames, cotangent, lengths, w_in, w_out, gain_pre, gain_mid, w_depth):
    sections = lax.axis_size("section")
    section_index = lax.axis_index("section")
    micro_count = frames.shape[0]
    frames_len = frames.shape[2]
    model_width = frames.shape[3]
    slots = micro_count + SKEW * (sections - 1)
    scale = 1.0 / math.sqrt(
        micro_count * frames_len * lax.axis_size("fsdp") * lax.axis_size("batch")
    )
    w_in_full, w_out_full = gather_weights(w_in[0], w_out[0])
    taps = w_depth.shape[1]
    params = jnp.concatenate(
        [
            w_depth[0],
            jnp.zeros((GAIN_A - taps, model_width), jnp.float32),
            gain_pre,
            jnp.zeros((GAIN_B - GAIN_A - 1, model_width), jnp.float32),
            gain_mid,
            jnp.zeros((PARAM_ROWS - GAIN_B - 1, model_width), jnp.float32),
        ],
        axis=0,
    )
    frame_rows = frames.reshape(micro_count, frames_len, model_width)
    cotangent_rows = cotangent.reshape(micro_count, frames_len, model_width)

    def info_table(place):
        micro_index = jnp.arange(slots, dtype=jnp.int32) - SKEW * place
        active = (micro_index >= 0) & (micro_index < micro_count)
        slot = jnp.clip(micro_index, 0, micro_count - 1)
        first = jnp.broadcast_to(place == 0, active.shape)
        valid = jnp.take(lengths[:, 0], slot)
        return jnp.stack([slot, active.astype(jnp.int32), first.astype(jnp.int32), valid], axis=1)

    def active_at(slot, flipped):
        places = [p for p in range(sections) if 0 <= slot - SKEW * p < micro_count]
        return [sections - 1 - p for p in places] if flipped else places

    blank = jnp.zeros((frames_len, model_width), jnp.bfloat16)
    pending = [blank] * SKEW
    table = info_table(section_index)
    saved = None
    for slot in range(slots):
        outgoing, *saved = forward_stage(
            table[slot], pending.pop(0), frame_rows, w_in_full, w_out_full, params, saved, taps
        )
        pending.append(send_active(outgoing, active_at(slot, False), 1))
    x_all, proj_all, swish_all, value_all, gate_all, mid_all, inv_all = saved
    kept = (x_all, value_all, gate_all, mid_all, inv_all)
    pending = [blank] * SKEW
    table = info_table(sections - 1 - section_index)
    grads = None
    for slot in range(slots):
        outgoing, *grads = backward_stage(
            table[slot], pending.pop(0), cotangent_rows, w_in_full, w_out_full, params, kept,
            grads, taps,
        )
        pending.append(send_active(outgoing, active_at(slot, True), -1))
    input_all, grad_all, up_all, small_all = grads
    total_rows = micro_count * frames_len
    parts, unused, width = w_in_full.shape
    proj_rows = proj_all.reshape(total_rows, model_width)
    grad_rows = grad_all.reshape(total_rows, 2 * model_width)
    swish_rows = swish_all.reshape(total_rows, model_width)
    upstream_rows = up_all.reshape(total_rows, model_width)

    def term(left, right):
        return lax.dot_general(
            left, right, (((0,), (0,)), ((), ())), preferred_element_type=jnp.float32
        ).astype(jnp.bfloat16)

    term_in = jnp.stack(
        [term(proj_rows, grad_rows[:, part * width : (part + 1) * width]) for part in range(parts)]
    )
    term_out = term(swish_rows, upstream_rows)
    small_rows = jnp.sum(small_all, axis=0)
    small = jnp.concatenate(
        [
            small_rows[GAIN_A : GAIN_A + 1],
            small_rows[GAIN_B : GAIN_B + 1],
            small_rows[:taps],
        ],
        axis=0,
    )
    grad_in, grad_out, small_total = reduce_weights(term_in, term_out, small, scale)
    input_grads = input_all.reshape(1, micro_count, 1, frames_len, model_width)
    return (
        input_grads,
        grad_in[None],
        grad_out[None],
        small_total[0:1],
        small_total[1:2],
        small_total[2:][None],
    )


def solution(mesh):
    in_specs = (
        P(None, ("fsdp", "batch"), None, None),
        P(None, ("fsdp", "batch"), None, None),
        P(None, ("fsdp", "batch")),
        P("section", "fsdp", None),
        P("section", "fsdp", None),
        P("section", None),
        P("section", None),
        P("section", None, None),
    )
    out_specs = (
        P("section", None, ("fsdp", "batch"), None, None),
        P("section", "fsdp", None),
        P("section", "fsdp", None),
        P("section", None),
        P("section", None),
        P("section", None, None),
    )
    return jax.shard_map(local, mesh=mesh, in_specs=in_specs, out_specs=out_specs, check_vma=False)
```

```python
import functools
import math

import jax
import jax.numpy as jnp
from jax import lax
from jax.experimental import pallas as pl
from jax.experimental.pallas import tpu as pltpu
from jax.sharding import PartitionSpec as P

epsilon = 1e-05
LANES = 128
SUBLANES = 8
MARGIN = 16
GAIN_A = 32
GAIN_B = 40
PARAM_ROWS = 48
SKEW = 2
IN_PARTS = 6
VMEM_LIMIT = 64 * 1024 * 1024 - 64 * 1024
PAIR = 2


def rotate(x, axis, by):
    peers = lax.axis_size(axis)
    return lax.ppermute(x, axis, [(i, (i + by) % peers) for i in range(peers)])


def swap_bit(x, bit):
    peers = lax.axis_size("fsdp")
    return lax.ppermute(x, "fsdp", [(i, i ^ bit) for i in range(peers)])


def ring_position():
    index = lax.axis_index("fsdp")
    return index // PAIR, index % PAIR


def pick(stacked, index, axis=0):
    return lax.dynamic_index_in_dim(stacked, index, axis, keepdims=False)


def column_parts(x, width):
    return [x[:, start : start + width] for start in range(0, x.shape[1], width)]


def ring_gather(payload, place, far_split):
    ring = lax.axis_size("fsdp") // PAIR
    half = ring // 2
    up, down = payload, payload
    for hop in range(1, half):
        up = rotate(up, "fsdp", PAIR)
        down = rotate(down, "fsdp", -PAIR)
        place(up, ring - hop)
        place(down, hop)
    far_up = rotate(up[:far_split], "fsdp", PAIR)
    far_down = rotate(down[far_split:], "fsdp", -PAIR)
    place(jnp.concatenate([far_up, far_down], axis=0), half)


def gather_weights(w_in, w_out):
    quarters = lax.axis_size("batch")
    ring = lax.axis_size("fsdp") // PAIR
    at, side = ring_position()
    rows, width = w_in.shape[0], w_in.shape[1] // IN_PARTS
    out_parts = w_out.shape[1] // width
    rest = IN_PARTS - quarters
    mine = lax.dynamic_slice_in_dim(w_in, lax.axis_index("batch") * width, width, 1)
    first = jnp.stack([mine] + column_parts(w_in, width)[quarters:])
    other = swap_bit(first, 1)
    both = jnp.where(side == 0, jnp.stack([first, other], 1), jnp.stack([other, first], 1))
    shared = jnp.zeros((ring, PAIR, rows, width), w_in.dtype)
    whole = jnp.zeros((rest, ring, PAIR, rows, width), w_in.dtype)
    out = jnp.zeros((out_parts, ring, PAIR, rows, width), w_in.dtype)

    def place_shared(piece, offset):
        nonlocal shared
        spot = ((at + offset) % ring, 0, 0, 0)
        shared = lax.dynamic_update_slice(shared, piece[None], spot)

    def place_out(piece, offset, where):
        nonlocal out
        spot = (0, (at + offset) % ring, where, 0, 0)
        out = lax.dynamic_update_slice(out, piece[:, None, None], spot)

    def place_rest(piece, offset):
        nonlocal whole
        pair = piece[: rest * PAIR].reshape(rest, 1, PAIR, rows, width)
        whole = lax.dynamic_update_slice(whole, pair, (0, (at + offset) % ring, 0, 0, 0))
        own = piece[rest * PAIR :]
        place_out(own, offset, side)
        place_out(swap_bit(own, 1), offset, 1 - side)

    place_shared(both[0], 0)
    ring_gather(both[0], place_shared, 1)
    payload = jnp.concatenate(
        [both[1:].reshape(rest * PAIR, rows, width), jnp.stack(column_parts(w_out, width))]
    )
    place_rest(payload, 0)
    ring_gather(payload, place_rest, (rest * PAIR + out_parts) // 2)
    depth = ring * PAIR * rows
    shared = lax.all_gather(shared.reshape(depth, width), "batch", axis=0, tiled=False)
    return shared, whole.reshape(rest, depth, width), out.reshape(out_parts, depth, width)


def ring_scatter(term_at, far_split):
    ring = lax.axis_size("fsdp") // PAIR
    half = ring // 2
    far = term_at(half)
    kind = far.dtype
    up = rotate(far[:far_split], "fsdp", PAIR).astype(jnp.float32)
    down = rotate(far[far_split:], "fsdp", -PAIR).astype(jnp.float32)
    for hop in range(half - 1, 0, -1):
        mine_up = term_at(hop).astype(jnp.float32)
        mine_down = term_at(ring - hop).astype(jnp.float32)
        if hop == half - 1:
            up = jnp.concatenate([mine_up[:far_split] + up, mine_up[far_split:]])
            down = jnp.concatenate([mine_down[:far_split], mine_down[far_split:] + down])
        else:
            up = mine_up + up
            down = mine_down + down
        up = rotate(up.astype(kind), "fsdp", PAIR).astype(jnp.float32)
        down = rotate(down.astype(kind), "fsdp", -PAIR).astype(jnp.float32)
    return term_at(0).astype(jnp.float32) + up + down


def keep_side(total, kind):
    side = lax.axis_index("fsdp") % PAIR
    mine = jnp.where(side == 0, total[:, 0], total[:, 1])
    theirs = jnp.where(side == 0, total[:, 1], total[:, 0])
    return mine + swap_bit(theirs.astype(kind), 1).astype(jnp.float32)


def batch_copies(x):
    return x, rotate(x, "batch", 1), rotate(x, "batch", 2), rotate(x, "batch", 3)


def batch_order(copies):
    quarters = len(copies)
    here = lax.axis_index("batch")
    stacked = jnp.stack(copies)
    return [pick(stacked, (here + quarters - part) % quarters) for part in range(quarters)]


def sum_batch(x):
    own, left, far, right = (part.astype(jnp.float32) for part in batch_copies(x))
    return (own + far) + (left + right)


def sum_small(small):
    quarters = lax.axis_size("batch")
    here = lax.axis_index("batch")
    width = small.shape[1] // quarters
    pieces = jnp.stack(column_parts(small, width))
    mine = pick(pieces, here)
    for by in range(1, quarters):
        mine = mine + rotate(pick(pieces, (here + by) % quarters), "batch", by)
    bit = 1
    while bit < lax.axis_size("fsdp"):
        mine = mine + swap_bit(mine, bit)
        bit *= 2
    return jnp.concatenate(batch_order(batch_copies(mine)), axis=1)


def reduce_weights(shared, rest, out, small, scale):
    ring = lax.axis_size("fsdp") // PAIR
    at, side = ring_position()
    kind = shared.dtype
    quarters, depth, width = shared.shape
    rows = depth // (ring * PAIR)
    split = (ring, PAIR, rows, width)
    shared_sum = lax.psum_scatter(shared, "batch", scatter_dimension=0, tiled=False).reshape(split)
    rest_pairs = rest.reshape((-1,) + split)
    out_pairs = out.reshape((-1,) + split)
    rest_parts, out_parts = rest_pairs.shape[0], out_pairs.shape[0]
    small_total = scale * sum_small(small)

    def out_for(offset, where):
        spot = pick(out_pairs, (at + offset) % ring, 1)
        return pick(spot, where, 1)

    def main_term(offset):
        pair = pick(rest_pairs, (at + offset) % ring, 1).reshape(-1, rows, width)
        given = swap_bit(out_for(offset, 1 - side), 1).astype(jnp.float32)
        own = (out_for(offset, side).astype(jnp.float32) + given).astype(kind)
        return jnp.concatenate([pair, own])

    total = ring_scatter(main_term, (rest_parts * PAIR + out_parts) // 2)
    rest_share = keep_side(
        total[: rest_parts * PAIR].reshape(rest_parts, PAIR, rows, width), kind
    )
    share = jnp.concatenate([rest_share, total[rest_parts * PAIR :]]).astype(kind)
    share = sum_batch(share)
    shared_total = ring_scatter(lambda offset: pick(shared_sum, (at + offset) % ring), 1)
    shared_share = keep_side(shared_total[None], kind)[0].astype(kind)
    in_parts = [part.astype(jnp.float32) for part in batch_order(batch_copies(shared_share))]
    grad_in = jnp.concatenate(in_parts + [share[part] for part in range(rest_parts)], axis=1)
    grad_out = jnp.concatenate([share[rest_parts + part] for part in range(out_parts)], axis=1)
    return scale * grad_in, scale * grad_out, small_total


def layer_stats(values):
    mean_value = jnp.mean(values, axis=-1, keepdims=True)
    centred = values - mean_value
    inv_scale = lax.rsqrt(jnp.mean(centred * centred, axis=-1, keepdims=True) + epsilon)
    return centred * inv_scale, inv_scale


def norm_grad(upstream, normed, inv_scale):
    return (
        upstream
        - jnp.mean(upstream, axis=-1, keepdims=True)
        - normed * jnp.mean(upstream * normed, axis=-1, keepdims=True)
    ) * inv_scale


def rows_by(left, right):
    return jnp.dot(left, right, preferred_element_type=jnp.float32)


def rows_back(left, right):
    return lax.dot_general(
        left, right, (((1,), (1,)), ((), ())), preferred_element_type=jnp.float32
    )


def write_shifts(shifts, padded):
    span = shifts.shape[1]

    def shift(lanes):
        for by in range(SUBLANES):
            shifts[by, :, lanes] = padded[pl.ds(by, span), lanes]

    each_lane_block(padded.shape[1], shift)


def clear_margins(padded, length):
    zeros = jnp.zeros((MARGIN, padded.shape[1]), jnp.float32)
    padded[pl.ds(0, MARGIN), :] = zeros
    padded[pl.ds(MARGIN + length, MARGIN), :] = zeros


def each_block(width, size, body):
    def step(block, carry):
        body(block, pl.ds(pl.multiple_of(block * size, size), size))
        return carry

    lax.fori_loop(0, width // size, step, 0)


def each_lane_block(width, body):
    each_block(width, LANES, lambda block, lanes: body(lanes))


def shifted(shifts, offset, length, lanes):
    start = offset // SUBLANES * SUBLANES
    return shifts[offset % SUBLANES, pl.ds(start, length), lanes]


def part_copy(source, index, target, part, sems, base):
    return pltpu.make_async_copy(source.at[index], target.at[part], sems.at[base + part])


def start_parts(shared, rest, target, sems, base):
    for part in range(shared.shape[0]):
        part_copy(shared, part, target, part, sems, base).start()
    for part in range(rest.shape[0]):
        part_copy(rest, part, target, shared.shape[0] + part, sems, base).start()


def forward_kernel(
    info, incoming, frames, w_shared, w_rest, w_out, params, *refs, taps, length, width, aliased
):
    refs = refs[aliased:]
    outgoing, x_all, proj_all, swish_all, value_all, gate_all, mid_all, inv_all = refs[:8]
    (
        x_v, w_in_v, w_out_v, params_v, proj_v, swish_v, value_v, gate_v, mid_v, inv_v,
        padded, shifts, conv_v, out_v, in_sems, out_sems,
    ) = refs[8:]
    slot, active, first, valid = info[0], info[1], info[2], info[3]
    parts = w_in_v.shape[0]
    half = taps // 2

    @pl.when(active == 1)
    def run():
        x_copy = pltpu.make_async_copy(incoming, x_v, in_sems.at[0])
        frame_copy = pltpu.make_async_copy(frames.at[slot], x_v, in_sems.at[0])

        @pl.when(first == 1)
        def from_frames():
            frame_copy.start()

        @pl.when(first == 0)
        def from_neighbour():
            x_copy.start()

        params_copy = pltpu.make_async_copy(params, params_v, in_sems.at[1])
        params_copy.start()
        start_parts(w_shared, w_rest, w_in_v, in_sems, 2)
        w_out_copy = pltpu.make_async_copy(w_out, w_out_v, in_sems.at[2 + parts])
        w_out_copy.start()
        saves = []

        def save(source, target):
            copy = pltpu.make_async_copy(source, target, out_sems.at[len(saves)])
            copy.start()
            saves.append(copy)

        clear_margins(padded, length)
        x_copy.wait()
        params_copy.wait()
        source = x_v[...].astype(jnp.float32)
        save(x_v, x_all.at[slot])
        normed_in, unused = layer_stats(source)
        proj_v[...] = (normed_in * params_v[pl.ds(GAIN_A, 1), :]).astype(jnp.bfloat16)
        save(proj_v, proj_all.at[slot])
        part_width = w_in_v.shape[2]

        def into_value(part, lanes):
            part_copy(w_shared, 0, w_in_v, part, in_sems, 2).wait()
            value_v[:, lanes] = rows_by(proj_v[...], w_in_v[part])

        def into_gate(block, lanes):
            part = block + parts // 2
            part_copy(w_shared, 0, w_in_v, part, in_sems, 2).wait()
            gate_v[:, lanes] = jax.nn.sigmoid(rows_by(proj_v[...], w_in_v[part]))

        each_block(width, part_width, into_value)
        each_block(width, part_width, into_gate)
        save(value_v, value_all.at[slot])
        save(gate_v, gate_all.at[slot])
        rows = lax.broadcasted_iota(jnp.int32, (length, width), 0)
        mask = (rows < valid).astype(jnp.float32)
        padded[pl.ds(MARGIN, length), :] = value_v[...] * gate_v[...] * mask
        write_shifts(shifts, padded)

        def convolve(lanes):
            total = jnp.zeros((length, LANES), jnp.float32)
            for tap in range(taps):
                weight = params_v[pl.ds(tap, 1), lanes]
                total = total + shifted(shifts, tap + MARGIN - half, length, lanes) * weight
            conv_v[:, lanes] = total

        each_lane_block(width, convolve)
        normed_mid, inv_mid = layer_stats(conv_v[...])
        mid_v[...] = normed_mid
        inv_v[...] = jnp.broadcast_to(inv_mid, inv_v.shape)
        save(mid_v, mid_all.at[slot])
        save(inv_v, inv_all.at[slot])
        scaled_mid = normed_mid * params_v[pl.ds(GAIN_B, 1), :]
        swish_v[...] = (scaled_mid * jax.nn.sigmoid(scaled_mid)).astype(jnp.bfloat16)
        save(swish_v, swish_all.at[slot])
        w_out_copy.wait()

        def into_out(block, lanes):
            source = x_v[:, lanes].astype(jnp.float32)
            out_v[:, lanes] = (source + rows_by(swish_v[...], w_out_v[block])).astype(jnp.bfloat16)

        each_block(width, part_width, into_out)
        save(out_v, outgoing)
        for copy in saves:
            copy.wait()


def backward_kernel(
    info, incoming, cotangent, w_shared, w_rest, w_out, params,
    x_all, value_all, gate_all, mid_all, inv_all, *refs, taps, length, width, aliased
):
    refs = refs[aliased:]
    outgoing, input_all, grad_all, up_all, small_all = refs[:5]
    (
        u_v, w_in_v, w_out_v, params_v, x_v, value_v, gate_v, mid_v, inv_v,
        padded, shifts, padded_grad, shifts_grad, conv_v, grad_v, small_v, out_v,
        in_sems, out_sems,
    ) = refs[5:]
    slot, active, first, valid = info[0], info[1], info[2], info[3]
    parts = w_in_v.shape[0]
    half = taps // 2

    @pl.when(active == 1)
    def run():
        u_copy = pltpu.make_async_copy(incoming, u_v, in_sems.at[0])
        given_copy = pltpu.make_async_copy(cotangent.at[slot], u_v, in_sems.at[0])

        @pl.when(first == 1)
        def from_cotangent():
            given_copy.start()

        @pl.when(first == 0)
        def from_neighbour():
            u_copy.start()

        w_out_copy = pltpu.make_async_copy(w_out, w_out_v, in_sems.at[1])
        w_out_copy.start()
        loads = []
        for number, (source, target) in enumerate((
            (params, params_v),
            (value_all.at[slot], value_v),
            (gate_all.at[slot], gate_v),
            (mid_all.at[slot], mid_v),
            (inv_all.at[slot], inv_v),
            (x_all.at[slot], x_v),
        )):
            copy = pltpu.make_async_copy(source, target, in_sems.at[2 + number])
            copy.start()
            loads.append(copy)
        start_parts(w_shared, w_rest, w_in_v, in_sems, 8)
        saves = []

        def save(source, target):
            copy = pltpu.make_async_copy(source, target, out_sems.at[len(saves)])
            copy.start()
            saves.append(copy)

        clear_margins(padded, length)
        clear_margins(padded_grad, length)
        for copy in loads:
            copy.wait()
        rows = lax.broadcasted_iota(jnp.int32, (length, width), 0)
        mask = (rows < valid).astype(jnp.float32)
        padded[pl.ds(MARGIN, length), :] = value_v[...] * gate_v[...] * mask
        write_shifts(shifts, padded)
        u_copy.wait()
        save(u_v, up_all.at[slot])
        w_out_copy.wait()
        part_width = w_in_v.shape[2]
        conv_v[...] = jnp.zeros_like(conv_v)

        def into_swish(block, lanes):
            conv_v[...] += rows_back(u_v[:, lanes], w_out_v[block])

        each_block(width, part_width, into_swish)
        swish_grad = conv_v[...]
        normed_mid = mid_v[...]
        gain_b = params_v[pl.ds(GAIN_B, 1), :]
        scaled_mid = normed_mid * gain_b
        sigmoid_mid = jax.nn.sigmoid(scaled_mid)
        scaled_grad = swish_grad * (
            sigmoid_mid + scaled_mid * sigmoid_mid * (1.0 - sigmoid_mid)
        )
        small_v[pl.ds(GAIN_B, 1), :] = jnp.sum(scaled_grad * normed_mid, axis=0, keepdims=True)
        conv_grad = norm_grad(scaled_grad * gain_b, normed_mid, inv_v[:, :1])
        padded_grad[pl.ds(MARGIN, length), :] = conv_grad
        write_shifts(shifts_grad, padded_grad)

        def convolve(lanes):
            total = jnp.zeros((length, LANES), jnp.float32)
            for tap in range(taps):
                weight = params_v[pl.ds(tap, 1), lanes]
                total = total + shifted(shifts_grad, MARGIN + half - tap, length, lanes) * weight
            conv_v[:, lanes] = total

        each_lane_block(width, convolve)

        def correlate(lanes):
            given = padded_grad[pl.ds(MARGIN, length), lanes]
            for tap in range(taps):
                product = given * shifted(shifts, tap + MARGIN - half, length, lanes)
                small_v[pl.ds(tap, 1), lanes] = jnp.sum(product, axis=0, keepdims=True)

        each_lane_block(width, correlate)
        gated_grad = conv_v[...] * mask
        glu_gate = gate_v[...]
        grad_v[:, :width] = (gated_grad * glu_gate).astype(jnp.bfloat16)
        grad_v[:, width:] = (
            gated_grad * value_v[...] * glu_gate * (1.0 - glu_gate)
        ).astype(jnp.bfloat16)
        save(grad_v, grad_all.at[slot])
        conv_v[...] = jnp.zeros_like(conv_v)

        def into_input(part, lanes):
            part_copy(w_shared, 0, w_in_v, part, in_sems, 8).wait()
            conv_v[...] += rows_back(grad_v[:, lanes], w_in_v[part])

        each_block(2 * width, part_width, into_input)
        input_side = conv_v[...]
        normed_in, inv_in = layer_stats(x_v[...].astype(jnp.float32))
        small_v[pl.ds(GAIN_A, 1), :] = jnp.sum(input_side * normed_in, axis=0, keepdims=True)
        save(small_v, small_all.at[slot])
        gain_a = params_v[pl.ds(GAIN_A, 1), :]
        out_v[...] = (
            u_v[...].astype(jnp.float32) + norm_grad(input_side * gain_a, normed_in, inv_in)
        ).astype(jnp.bfloat16)
        save(out_v, outgoing)
        save(out_v, input_all.at[slot])
        for copy in saves:
            copy.wait()


def stage_call(kernel, scratch, info, inputs, out_shapes, buffers, taps, length, width, cost, sems):
    anywhere = pl.BlockSpec(memory_space=pl.ANY)
    aliases = {}
    operands = list(inputs)
    aliased = 0
    if buffers is not None:
        aliased = len(buffers)
        aliases = {1 + len(inputs) + number: 1 + number for number in range(aliased)}
        operands += list(buffers)
    in_sems, out_sems = sems
    return pl.pallas_call(
        functools.partial(kernel, taps=taps, length=length, width=width, aliased=aliased),
        grid_spec=pltpu.PrefetchScalarGridSpec(
            num_scalar_prefetch=1,
            grid=(),
            in_specs=[anywhere] * len(operands),
            out_specs=[anywhere] * len(out_shapes),
            scratch_shapes=list(scratch)
            + [pltpu.SemaphoreType.DMA((in_sems,)), pltpu.SemaphoreType.DMA((out_sems,))],
        ),
        out_shape=out_shapes,
        input_output_aliases=aliases,
        compiler_params=pltpu.CompilerParams(vmem_limit_bytes=VMEM_LIMIT),
        cost_estimate=cost,
    )(info, *operands)


def stage_cost(length, width):
    return pl.CostEstimate(
        flops=6 * length * width * width,
        transcendentals=2 * length * width,
        bytes_accessed=6 * width * width,
    )


def forward_stage(info, incoming, frames, weights, params, buffers, taps):
    micro, length, width = frames.shape
    f32, bf16 = jnp.float32, jnp.bfloat16
    shape = jax.ShapeDtypeStruct
    outs = [shape((length, width), bf16)] + [
        shape((micro, length, width), dtype) for dtype in (bf16, bf16, bf16, f32, f32, f32)
    ] + [shape((micro, length, LANES), f32)]
    rows = functools.partial(pltpu.VMEM, (length, width))
    span = length + 2 * MARGIN
    scratch = [
        rows(bf16), pltpu.VMEM((IN_PARTS,) + weights[2].shape[1:], bf16), pltpu.VMEM(weights[2].shape, bf16),
        pltpu.VMEM(params.shape, f32), rows(bf16), rows(bf16), rows(f32), rows(f32), rows(f32),
        pltpu.VMEM((length, LANES), f32), pltpu.VMEM((span, width), f32),
        pltpu.VMEM((SUBLANES, span - SUBLANES, width), f32), rows(f32), rows(bf16),
    ]
    return stage_call(
        forward_kernel, scratch, info, (incoming, frames, *weights, params), outs, buffers,
        taps, length, width, stage_cost(length, width), (3 + IN_PARTS, 8),
    )


def backward_stage(info, incoming, cotangent, weights, params, saved, buffers, taps):
    micro, length, width = cotangent.shape
    f32, bf16 = jnp.float32, jnp.bfloat16
    shape = jax.ShapeDtypeStruct
    outs = [
        shape((length, width), bf16), shape((micro, length, width), bf16),
        shape((micro, length, 2 * width), bf16), shape((micro, length, width), bf16),
        shape((micro,) + params.shape, f32),
    ]
    rows = functools.partial(pltpu.VMEM, (length, width))
    span = length + 2 * MARGIN
    lifted = pltpu.VMEM((SUBLANES, span - SUBLANES, width), f32)
    scratch = [
        rows(bf16), pltpu.VMEM((IN_PARTS,) + weights[2].shape[1:], bf16), pltpu.VMEM(weights[2].shape, bf16),
        pltpu.VMEM(params.shape, f32), rows(bf16), rows(f32), rows(f32), rows(f32),
        pltpu.VMEM((length, LANES), f32), pltpu.VMEM((span, width), f32), lifted,
        pltpu.VMEM((span, width), f32), lifted, rows(f32),
        pltpu.VMEM((length, 2 * width), bf16), pltpu.VMEM(params.shape, f32), rows(bf16),
    ]
    return stage_call(
        backward_kernel, scratch, info, (incoming, cotangent, *weights, params) + tuple(saved),
        outs, buffers, taps, length, width, stage_cost(length, width), (8 + IN_PARTS, 5),
    )


def send_active(x, senders, by):
    pairs = [(s, s + by) for s in senders if 0 <= s + by < lax.axis_size("section")]
    return lax.ppermute(x, "section", pairs)


def local(frames, cotangent, lengths, w_in, w_out, gain_pre, gain_mid, w_depth):
    sections = lax.axis_size("section")
    section_index = lax.axis_index("section")
    micro_count = frames.shape[0]
    frames_len = frames.shape[2]
    model_width = frames.shape[3]
    slots = micro_count + SKEW * (sections - 1)
    scale = 1.0 / math.sqrt(
        micro_count * frames_len * lax.axis_size("fsdp") * lax.axis_size("batch")
    )
    weights = gather_weights(w_in[0], w_out[0])
    taps = w_depth.shape[1]
    params = jnp.concatenate(
        [
            w_depth[0],
            jnp.zeros((GAIN_A - taps, model_width), jnp.float32),
            gain_pre,
            jnp.zeros((GAIN_B - GAIN_A - 1, model_width), jnp.float32),
            gain_mid,
            jnp.zeros((PARAM_ROWS - GAIN_B - 1, model_width), jnp.float32),
        ],
        axis=0,
    )
    frame_rows = frames.reshape(micro_count, frames_len, model_width)
    cotangent_rows = cotangent.reshape(micro_count, frames_len, model_width)

    def info_table(place):
        micro_index = jnp.arange(slots, dtype=jnp.int32) - SKEW * place
        active = (micro_index >= 0) & (micro_index < micro_count)
        slot = jnp.clip(micro_index, 0, micro_count - 1)
        first = jnp.broadcast_to(place == 0, active.shape)
        valid = jnp.take(lengths[:, 0], slot)
        return jnp.stack([slot, active.astype(jnp.int32), first.astype(jnp.int32), valid], axis=1)

    def active_at(slot, flipped):
        places = [p for p in range(sections) if 0 <= slot - SKEW * p < micro_count]
        return [sections - 1 - p for p in places] if flipped else places

    blank = jnp.zeros((frames_len, model_width), jnp.bfloat16)
    pending = [blank] * SKEW
    table = info_table(section_index)
    saved = None
    for slot in range(slots):
        outgoing, *saved = forward_stage(
            table[slot], pending.pop(0), frame_rows, weights, params, saved, taps
        )
        pending.append(send_active(outgoing, active_at(slot, False), 1))
    x_all, proj_all, swish_all, value_all, gate_all, mid_all, inv_all = saved
    kept = (x_all, value_all, gate_all, mid_all, inv_all)
    pending = [blank] * SKEW
    table = info_table(sections - 1 - section_index)
    grads = None
    for slot in range(slots):
        outgoing, *grads = backward_stage(
            table[slot], pending.pop(0), cotangent_rows, weights, params, kept,
            grads, taps,
        )
        pending.append(send_active(outgoing, active_at(slot, True), -1))
    input_all, grad_all, up_all, small_all = grads
    total_rows = micro_count * frames_len
    width = weights[2].shape[2]
    quarters = weights[0].shape[0]
    proj_rows = proj_all.reshape(total_rows, model_width)
    grad_rows = grad_all.reshape(total_rows, 2 * model_width)
    swish_rows = swish_all.reshape(total_rows, model_width)
    upstream_rows = up_all.reshape(total_rows, model_width)

    def term(left, right):
        return lax.dot_general(
            left, right, (((0,), (0,)), ((), ())), preferred_element_type=jnp.float32
        ).astype(jnp.bfloat16)

    def terms(left, right, parts):
        return jnp.stack(
            [term(left, right[:, part * width : (part + 1) * width]) for part in parts]
        )

    shared_terms = terms(proj_rows, grad_rows, range(quarters))
    rest_terms = terms(proj_rows, grad_rows, range(quarters, IN_PARTS))
    out_terms = terms(swish_rows, upstream_rows, range(weights[2].shape[0]))
    small_rows = jnp.sum(small_all, axis=0)
    small = jnp.concatenate(
        [
            small_rows[GAIN_A : GAIN_A + 1],
            small_rows[GAIN_B : GAIN_B + 1],
            small_rows[:taps],
        ],
        axis=0,
    )
    grad_in, grad_out, small_total = reduce_weights(
        shared_terms, rest_terms, out_terms, small, scale
    )
    input_grads = input_all.reshape(1, micro_count, 1, frames_len, model_width)
    return (
        input_grads,
        grad_in[None],
        grad_out[None],
        small_total[0:1],
        small_total[1:2],
        small_total[2:][None],
    )


def solution(mesh):
    in_specs = (
        P(None, ("fsdp", "batch"), None, None),
        P(None, ("fsdp", "batch"), None, None),
        P(None, ("fsdp", "batch")),
        P("section", "fsdp", None),
        P("section", "fsdp", None),
        P("section", None),
        P("section", None),
        P("section", None, None),
    )
    out_specs = (
        P("section", None, ("fsdp", "batch"), None, None),
        P("section", "fsdp", None),
        P("section", "fsdp", None),
        P("section", None),
        P("section", None),
        P("section", None, None),
    )
    return jax.shard_map(local, mesh=mesh, in_specs=in_specs, out_specs=out_specs, check_vma=False)
```

```python
import functools
import math

import jax
import jax.numpy as jnp
from jax import lax
from jax.experimental import pallas as pl
from jax.experimental.pallas import tpu as pltpu
from jax.sharding import PartitionSpec as P

epsilon = 1e-05
LANES = 128
SUBLANES = 8
MARGIN = 16
GAIN_A = 32
GAIN_B = 40
PARAM_ROWS = 48
SKEW = 2
IN_PARTS = 6
SMALL_A = 0
SMALL_B = 8
LARGEST = 3.0e38
VMEM_LIMIT = 64 * 1024 * 1024 - 64 * 1024
PAIR = 2


def rotate(x, axis, by):
    peers = lax.axis_size(axis)
    return lax.ppermute(x, axis, [(i, (i + by) % peers) for i in range(peers)])


def swap_bit(x, bit):
    peers = lax.axis_size("fsdp")
    return lax.ppermute(x, "fsdp", [(i, i ^ bit) for i in range(peers)])


def ring_position():
    index = lax.axis_index("fsdp")
    return index // PAIR, index % PAIR


def pick(stacked, index, axis=0):
    return lax.dynamic_index_in_dim(stacked, index, axis, keepdims=False)


def after(x):
    value = jnp.abs(x.reshape(-1)[0].astype(jnp.float32))
    return jnp.where(value <= LARGEST, 0, 1).astype(jnp.int32)


def column_parts(x, width):
    return [x[:, start : start + width] for start in range(0, x.shape[1], width)]


def ring_gather(payload, place, far_split):
    ring = lax.axis_size("fsdp") // PAIR
    half = ring // 2
    up, down = payload, payload
    for hop in range(1, half):
        up = rotate(up, "fsdp", PAIR)
        down = rotate(down, "fsdp", -PAIR)
        place(up, ring - hop)
        place(down, hop)
    far_up = rotate(up[:far_split], "fsdp", PAIR)
    far_down = rotate(down[far_split:], "fsdp", -PAIR)
    place(jnp.concatenate([far_up, far_down], axis=0), half)


def gather_weights(w_in, w_out):
    quarters = lax.axis_size("batch")
    ring = lax.axis_size("fsdp") // PAIR
    at, side = ring_position()
    rows, width = w_in.shape[0], w_in.shape[1] // IN_PARTS
    out_parts = w_out.shape[1] // width
    rest = IN_PARTS - quarters
    mine = lax.dynamic_slice_in_dim(w_in, lax.axis_index("batch") * width, width, 1)
    first = jnp.stack([mine] + column_parts(w_in, width)[quarters:])
    other = swap_bit(first, 1)
    both = jnp.where(side == 0, jnp.stack([first, other], 1), jnp.stack([other, first], 1))
    shared = jnp.zeros((ring, PAIR, rows, width), w_in.dtype)
    whole = jnp.zeros((rest, ring, PAIR, rows, width), w_in.dtype)
    out = jnp.zeros((out_parts, ring, PAIR, rows, width), w_in.dtype)

    def place_shared(piece, offset):
        nonlocal shared
        spot = ((at + offset) % ring, 0, 0, 0)
        shared = lax.dynamic_update_slice(shared, piece[None], spot)

    def place_out(piece, offset, where):
        nonlocal out
        spot = (0, (at + offset) % ring, where, 0, 0)
        out = lax.dynamic_update_slice(out, piece[:, None, None], spot)

    def place_rest(piece, offset):
        nonlocal whole
        pair = piece[: rest * PAIR].reshape(rest, 1, PAIR, rows, width)
        whole = lax.dynamic_update_slice(whole, pair, (0, (at + offset) % ring, 0, 0, 0))
        own = piece[rest * PAIR :]
        place_out(own, offset, side)
        place_out(swap_bit(own, 1), offset, 1 - side)

    place_shared(both[0], 0)
    ring_gather(both[0], place_shared, 1)
    payload = jnp.concatenate(
        [both[1:].reshape(rest * PAIR, rows, width), jnp.stack(column_parts(w_out, width))]
    )
    place_rest(payload, 0)
    ring_gather(payload, place_rest, (rest * PAIR + out_parts) // 2)
    depth = ring * PAIR * rows
    shared = lax.all_gather(shared.reshape(depth, width), "batch", axis=0, tiled=False)
    return shared, whole.reshape(rest, depth, width), out.reshape(out_parts, depth, width)


def ring_scatter(term_at, far_split, prepare=lambda hop, tie: None):
    ring = lax.axis_size("fsdp") // PAIR
    half = ring // 2
    far = term_at(half)
    kind = far.dtype
    prepare(half - 1, far)
    up = rotate(far[:far_split], "fsdp", PAIR).astype(jnp.float32)
    down = rotate(far[far_split:], "fsdp", -PAIR).astype(jnp.float32)
    for hop in range(half - 1, 0, -1):
        mine_up = term_at(hop).astype(jnp.float32)
        mine_down = term_at(ring - hop).astype(jnp.float32)
        if hop == half - 1:
            up = jnp.concatenate([mine_up[:far_split] + up, mine_up[far_split:]])
            down = jnp.concatenate([mine_down[:far_split], mine_down[far_split:] + down])
        else:
            up = mine_up + up
            down = mine_down + down
        up = up.astype(kind)
        down = down.astype(kind)
        prepare(hop - 1, up)
        up = rotate(up, "fsdp", PAIR).astype(jnp.float32)
        down = rotate(down, "fsdp", -PAIR).astype(jnp.float32)
    return term_at(0).astype(jnp.float32) + up + down


def keep_side(total, kind):
    side = lax.axis_index("fsdp") % PAIR
    mine = jnp.where(side == 0, total[:, 0], total[:, 1])
    theirs = jnp.where(side == 0, total[:, 1], total[:, 0])
    return mine + swap_bit(theirs.astype(kind), 1).astype(jnp.float32)


def batch_copies(x):
    return x, rotate(x, "batch", 1), rotate(x, "batch", 2), rotate(x, "batch", 3)


def batch_order(copies):
    quarters = len(copies)
    here = lax.axis_index("batch")
    stacked = jnp.stack(copies)
    return [pick(stacked, (here + quarters - part) % quarters) for part in range(quarters)]


def sum_batch(x):
    own, left, far, right = (part.astype(jnp.float32) for part in batch_copies(x))
    return (own + far) + (left + right)


def small_steps(small):
    quarters = lax.axis_size("batch")
    here = lax.axis_index("batch")
    width = small.shape[1] // quarters
    pieces = jnp.stack(column_parts(small, width))
    tie = yield None
    mine = pick(pieces, here)
    for by in range(1, quarters):
        mine = mine + rotate(pick(pieces, (here + by) % quarters + tie), "batch", by)
    bit = 1
    while bit < lax.axis_size("fsdp"):
        tie = yield None
        mine = mine + swap_bit(mine + tie.astype(jnp.float32), bit)
        bit *= 2
    tie = yield None
    mine = mine + tie.astype(jnp.float32)
    yield jnp.concatenate(batch_order(batch_copies(mine)), axis=1)


def reduce_weights(shared, rest, out, small, scale):
    ring = lax.axis_size("fsdp") // PAIR
    at, side = ring_position()
    kind = shared.dtype
    quarters, depth, width = shared.shape
    rows = depth // (ring * PAIR)
    split = (ring, PAIR, rows, width)
    shared_sum = lax.psum_scatter(shared, "batch", scatter_dimension=0, tiled=False).reshape(split)
    rest_pairs = rest.reshape((-1,) + split)
    out_pairs = out.reshape((-1,) + split)
    rest_parts, out_parts = rest_pairs.shape[0], out_pairs.shape[0]
    steps = small_steps(small)
    next(steps)
    given = {}

    def out_for(offset, where):
        spot = pick(out_pairs, (at + offset) % ring, 1)
        return pick(spot, where, 1)

    def exchange(offsets, tie):
        theirs = jnp.concatenate([out_for(offset + tie, 1 - side) for offset in offsets])
        arrived = swap_bit(theirs, 1)
        for number, offset in enumerate(offsets):
            given[offset] = arrived[number * out_parts : (number + 1) * out_parts]

    def main_term(offset):
        pair = pick(rest_pairs, (at + offset) % ring, 1).reshape(-1, rows, width)
        extra = given[offset].astype(jnp.float32)
        own = (out_for(offset, side).astype(jnp.float32) + extra).astype(kind)
        return jnp.concatenate([pair, own])

    def prepare(hop, ready):
        tie = after(ready)
        exchange([hop, ring - hop] if hop else [0], tie)
        steps.send(tie)

    exchange([ring // 2], 0)
    total = ring_scatter(main_term, (rest_parts * PAIR + out_parts) // 2, prepare)
    steps.send(after(total))
    rest_share = keep_side(
        total[: rest_parts * PAIR].reshape(rest_parts, PAIR, rows, width), kind
    )
    share = jnp.concatenate([rest_share, total[rest_parts * PAIR :]]).astype(kind)
    small_total = scale * steps.send(after(share))
    share = sum_batch(share)
    shared_total = ring_scatter(lambda offset: pick(shared_sum, (at + offset) % ring), 1)
    shared_share = keep_side(shared_total[None], kind)[0].astype(kind)
    in_parts = [part.astype(jnp.float32) for part in batch_order(batch_copies(shared_share))]
    grad_in = jnp.concatenate(in_parts + [share[part] for part in range(rest_parts)], axis=1)
    grad_out = jnp.concatenate([share[rest_parts + part] for part in range(out_parts)], axis=1)
    return scale * grad_in, scale * grad_out, small_total


def layer_stats(values):
    mean_value = jnp.mean(values, axis=-1, keepdims=True)
    centred = values - mean_value
    inv_scale = lax.rsqrt(jnp.mean(centred * centred, axis=-1, keepdims=True) + epsilon)
    return centred * inv_scale, inv_scale


def norm_grad(upstream, normed, inv_scale):
    return (
        upstream
        - jnp.mean(upstream, axis=-1, keepdims=True)
        - normed * jnp.mean(upstream * normed, axis=-1, keepdims=True)
    ) * inv_scale


def rows_by(left, right):
    return jnp.dot(left, right, preferred_element_type=jnp.float32)


def rows_back(left, right):
    return lax.dot_general(
        left, right, (((1,), (1,)), ((), ())), preferred_element_type=jnp.float32
    )


def write_shifts(shifts, padded):
    span = shifts.shape[1]

    def shift(lanes):
        for by in range(SUBLANES):
            shifts[by, :, lanes] = padded[pl.ds(by, span), lanes]

    each_lane_block(padded.shape[1], shift)


def clear_margins(padded, length):
    zeros = jnp.zeros((MARGIN, padded.shape[1]), jnp.float32)
    padded[pl.ds(0, MARGIN), :] = zeros
    padded[pl.ds(MARGIN + length, MARGIN), :] = zeros


def each_block(width, size, body):
    def step(block, carry):
        body(block, pl.ds(pl.multiple_of(block * size, size), size))
        return carry

    lax.fori_loop(0, width // size, step, 0)


def each_lane_block(width, body):
    each_block(width, LANES, lambda block, lanes: body(lanes))


def shifted(shifts, offset, length, lanes):
    start = offset // SUBLANES * SUBLANES
    return shifts[offset % SUBLANES, pl.ds(start, length), lanes]


def part_copy(source, index, target, part, sems, base):
    return pltpu.make_async_copy(source.at[index], target.at[part], sems.at[base + part])


def start_parts(shared, rest, target, sems, base):
    for part in range(shared.shape[0]):
        part_copy(shared, part, target, part, sems, base).start()
    for part in range(rest.shape[0]):
        part_copy(rest, part, target, shared.shape[0] + part, sems, base).start()


def forward_kernel(
    info, incoming, frames, w_shared, w_rest, w_out, params, *refs, taps, length, width, aliased
):
    refs = refs[aliased:]
    outgoing, x_all, proj_all, swish_all, value_all, gate_all, mid_all, inv_all = refs[:8]
    (
        x_v, w_in_v, w_out_v, params_v, proj_v, swish_v, value_v, gate_v, mid_v, inv_v,
        padded, shifts, conv_v, out_v, in_sems, out_sems,
    ) = refs[8:]
    slot, active, first, valid = info[0], info[1], info[2], info[3]
    parts = w_in_v.shape[0]
    half = taps // 2

    @pl.when(active == 1)
    def run():
        x_copy = pltpu.make_async_copy(incoming, x_v, in_sems.at[0])
        frame_copy = pltpu.make_async_copy(frames.at[slot], x_v, in_sems.at[0])

        @pl.when(first == 1)
        def from_frames():
            frame_copy.start()

        @pl.when(first == 0)
        def from_neighbour():
            x_copy.start()

        params_copy = pltpu.make_async_copy(params, params_v, in_sems.at[1])
        params_copy.start()
        start_parts(w_shared, w_rest, w_in_v, in_sems, 2)
        w_out_copy = pltpu.make_async_copy(w_out, w_out_v, in_sems.at[2 + parts])
        w_out_copy.start()
        saves = []

        def save(source, target):
            copy = pltpu.make_async_copy(source, target, out_sems.at[len(saves)])
            copy.start()
            saves.append(copy)

        clear_margins(padded, length)
        x_copy.wait()
        params_copy.wait()
        source = x_v[...].astype(jnp.float32)
        save(x_v, x_all.at[slot])
        normed_in, unused = layer_stats(source)
        proj_v[...] = (normed_in * params_v[pl.ds(GAIN_A, 1), :]).astype(jnp.bfloat16)
        save(proj_v, proj_all.at[slot])
        part_width = w_in_v.shape[2]

        def into_value(part, lanes):
            part_copy(w_shared, 0, w_in_v, part, in_sems, 2).wait()
            value_v[:, lanes] = rows_by(proj_v[...], w_in_v[part])

        def into_gate(block, lanes):
            part = block + parts // 2
            part_copy(w_shared, 0, w_in_v, part, in_sems, 2).wait()
            gate_v[:, lanes] = jax.nn.sigmoid(rows_by(proj_v[...], w_in_v[part]))

        each_block(width, part_width, into_value)
        each_block(width, part_width, into_gate)
        save(value_v, value_all.at[slot])
        save(gate_v, gate_all.at[slot])
        rows = lax.broadcasted_iota(jnp.int32, (length, width), 0)
        mask = (rows < valid).astype(jnp.float32)
        padded[pl.ds(MARGIN, length), :] = value_v[...] * gate_v[...] * mask
        write_shifts(shifts, padded)

        def convolve(lanes):
            total = jnp.zeros((length, LANES), jnp.float32)
            for tap in range(taps):
                weight = params_v[pl.ds(tap, 1), lanes]
                total = total + shifted(shifts, tap + MARGIN - half, length, lanes) * weight
            conv_v[:, lanes] = total

        each_lane_block(width, convolve)
        normed_mid, inv_mid = layer_stats(conv_v[...])
        mid_v[...] = normed_mid
        inv_v[...] = jnp.broadcast_to(inv_mid, inv_v.shape)
        save(mid_v, mid_all.at[slot])
        save(inv_v, inv_all.at[slot])
        scaled_mid = normed_mid * params_v[pl.ds(GAIN_B, 1), :]
        swish_v[...] = (scaled_mid * jax.nn.sigmoid(scaled_mid)).astype(jnp.bfloat16)
        save(swish_v, swish_all.at[slot])
        w_out_copy.wait()

        def into_out(block, lanes):
            source = x_v[:, lanes].astype(jnp.float32)
            out_v[:, lanes] = (source + rows_by(swish_v[...], w_out_v[block])).astype(jnp.bfloat16)

        each_block(width, part_width, into_out)
        save(out_v, outgoing)
        for copy in saves:
            copy.wait()


def backward_kernel(
    info, incoming, cotangent, w_shared, w_rest, w_out, params,
    x_all, value_all, gate_all, mid_all, inv_all, *refs, taps, length, width, aliased
):
    refs = refs[aliased:]
    outgoing, input_all, grad_all, up_all, small_all, conv_all = refs[:6]
    (
        u_v, w_in_v, w_out_v, params_v, x_v, value_v, gate_v, mid_v, inv_v,
        padded_grad, shifts_grad, conv_v, grad_v, small_v, out_v,
        in_sems, out_sems,
    ) = refs[6:]
    slot, active, first, valid = info[0], info[1], info[2], info[3]
    parts = w_in_v.shape[0]
    half = taps // 2

    @pl.when(active == 1)
    def run():
        u_copy = pltpu.make_async_copy(incoming, u_v, in_sems.at[0])
        given_copy = pltpu.make_async_copy(cotangent.at[slot], u_v, in_sems.at[0])

        @pl.when(first == 1)
        def from_cotangent():
            given_copy.start()

        @pl.when(first == 0)
        def from_neighbour():
            u_copy.start()

        w_out_copy = pltpu.make_async_copy(w_out, w_out_v, in_sems.at[1])
        w_out_copy.start()
        loads = []
        for number, (source, target) in enumerate((
            (params, params_v),
            (value_all.at[slot], value_v),
            (gate_all.at[slot], gate_v),
            (mid_all.at[slot], mid_v),
            (inv_all.at[slot], inv_v),
            (x_all.at[slot], x_v),
        )):
            copy = pltpu.make_async_copy(source, target, in_sems.at[2 + number])
            copy.start()
            loads.append(copy)
        start_parts(w_shared, w_rest, w_in_v, in_sems, 8)
        saves = []

        def save(source, target):
            copy = pltpu.make_async_copy(source, target, out_sems.at[len(saves)])
            copy.start()
            saves.append(copy)

        clear_margins(padded_grad, length)
        small_v[...] = jnp.zeros_like(small_v)
        for copy in loads:
            copy.wait()
        rows = lax.broadcasted_iota(jnp.int32, (length, width), 0)
        mask = (rows < valid).astype(jnp.float32)
        u_copy.wait()
        save(u_v, up_all.at[slot])
        w_out_copy.wait()
        part_width = w_in_v.shape[2]
        conv_v[...] = jnp.zeros_like(conv_v)

        def into_swish(block, lanes):
            conv_v[...] += rows_back(u_v[:, lanes], w_out_v[block])

        each_block(width, part_width, into_swish)
        swish_grad = conv_v[...]
        normed_mid = mid_v[...]
        gain_b = params_v[pl.ds(GAIN_B, 1), :]
        scaled_mid = normed_mid * gain_b
        sigmoid_mid = jax.nn.sigmoid(scaled_mid)
        scaled_grad = swish_grad * (
            sigmoid_mid + scaled_mid * sigmoid_mid * (1.0 - sigmoid_mid)
        )
        small_v[pl.ds(SMALL_B, 1), :] = jnp.sum(scaled_grad * normed_mid, axis=0, keepdims=True)
        conv_grad = norm_grad(scaled_grad * gain_b, normed_mid, inv_v[:, :1])
        padded_grad[pl.ds(MARGIN, length), :] = conv_grad
        save(padded_grad.at[pl.ds(MARGIN, length), :], conv_all.at[slot])
        write_shifts(shifts_grad, padded_grad)

        def convolve(lanes):
            total = jnp.zeros((length, LANES), jnp.float32)
            for tap in range(taps):
                weight = params_v[pl.ds(tap, 1), lanes]
                total = total + shifted(shifts_grad, MARGIN + half - tap, length, lanes) * weight
            conv_v[:, lanes] = total

        each_lane_block(width, convolve)

        gated_grad = conv_v[...] * mask
        glu_gate = gate_v[...]
        grad_v[:, :width] = (gated_grad * glu_gate).astype(jnp.bfloat16)
        grad_v[:, width:] = (
            gated_grad * value_v[...] * glu_gate * (1.0 - glu_gate)
        ).astype(jnp.bfloat16)
        save(grad_v, grad_all.at[slot])
        conv_v[...] = jnp.zeros_like(conv_v)

        def into_input(part, lanes):
            part_copy(w_shared, 0, w_in_v, part, in_sems, 8).wait()
            conv_v[...] += rows_back(grad_v[:, lanes], w_in_v[part])

        each_block(2 * width, part_width, into_input)
        input_side = conv_v[...]
        normed_in, inv_in = layer_stats(x_v[...].astype(jnp.float32))
        small_v[pl.ds(SMALL_A, 1), :] = jnp.sum(input_side * normed_in, axis=0, keepdims=True)
        save(small_v, small_all.at[slot])
        gain_a = params_v[pl.ds(GAIN_A, 1), :]
        out_v[...] = (
            u_v[...].astype(jnp.float32) + norm_grad(input_side * gain_a, normed_in, inv_in)
        ).astype(jnp.bfloat16)
        save(out_v, outgoing)
        save(out_v, input_all.at[slot])
        for copy in saves:
            copy.wait()


def taps_kernel(valid, grads, values, gates, out, padded, shifts, *, taps, length, width):
    micro = pl.program_id(0)

    @pl.when(micro == 0)
    def clear():
        out[...] = jnp.zeros_like(out)
        clear_margins(padded, length)

    rows = lax.broadcasted_iota(jnp.int32, (length, width), 0)
    mask = (rows < valid[micro]).astype(jnp.float32)
    padded[pl.ds(MARGIN, length), :] = values[0] * gates[0] * mask
    write_shifts(shifts, padded)

    def correlate(lanes):
        given = grads[0, :, lanes]
        for tap in range(taps):
            product = given * shifted(shifts, tap + MARGIN - taps // 2, length, lanes)
            out[pl.ds(tap, 1), lanes] += jnp.sum(product, axis=0, keepdims=True)

    each_lane_block(width, correlate)


def taps_sums(valid, grads, values, gates, taps):
    micro, length, width = grads.shape
    span = length + 2 * MARGIN
    block = pl.BlockSpec((1, length, width), lambda index, valid: (index, 0, 0))
    return pl.pallas_call(
        functools.partial(taps_kernel, taps=taps, length=length, width=width),
        grid_spec=pltpu.PrefetchScalarGridSpec(
            num_scalar_prefetch=1,
            grid=(micro,),
            in_specs=[block] * 3,
            out_specs=pl.BlockSpec((GAIN_A, width), lambda index, valid: (0, 0)),
            scratch_shapes=[
                pltpu.VMEM((span, width), jnp.float32),
                pltpu.VMEM((SUBLANES, span - SUBLANES, width), jnp.float32),
            ],
        ),
        out_shape=jax.ShapeDtypeStruct((GAIN_A, width), jnp.float32),
        compiler_params=pltpu.CompilerParams(vmem_limit_bytes=32 * 1024 * 1024),
        cost_estimate=pl.CostEstimate(
            flops=2 * taps * micro * length * width,
            transcendentals=0,
            bytes_accessed=12 * micro * length * width,
        ),
    )(valid, grads, values, gates)


def stage_call(kernel, scratch, info, inputs, out_shapes, buffers, taps, length, width, cost, sems):
    anywhere = pl.BlockSpec(memory_space=pl.ANY)
    aliases = {}
    operands = list(inputs)
    aliased = 0
    if buffers is not None:
        aliased = len(buffers)
        aliases = {1 + len(inputs) + number: 1 + number for number in range(aliased)}
        operands += list(buffers)
    in_sems, out_sems = sems
    return pl.pallas_call(
        functools.partial(kernel, taps=taps, length=length, width=width, aliased=aliased),
        grid_spec=pltpu.PrefetchScalarGridSpec(
            num_scalar_prefetch=1,
            grid=(),
            in_specs=[anywhere] * len(operands),
            out_specs=[anywhere] * len(out_shapes),
            scratch_shapes=list(scratch)
            + [pltpu.SemaphoreType.DMA((in_sems,)), pltpu.SemaphoreType.DMA((out_sems,))],
        ),
        out_shape=out_shapes,
        input_output_aliases=aliases,
        compiler_params=pltpu.CompilerParams(vmem_limit_bytes=VMEM_LIMIT),
        cost_estimate=cost,
    )(info, *operands)


def stage_cost(length, width):
    return pl.CostEstimate(
        flops=6 * length * width * width,
        transcendentals=2 * length * width,
        bytes_accessed=6 * width * width,
    )


def forward_stage(info, incoming, frames, weights, params, buffers, taps):
    micro, length, width = frames.shape
    f32, bf16 = jnp.float32, jnp.bfloat16
    shape = jax.ShapeDtypeStruct
    outs = [shape((length, width), bf16)] + [
        shape((micro, length, width), dtype) for dtype in (bf16, bf16, bf16, f32, f32, f32)
    ] + [shape((micro, length, LANES), f32)]
    rows = functools.partial(pltpu.VMEM, (length, width))
    span = length + 2 * MARGIN
    scratch = [
        rows(bf16), pltpu.VMEM((IN_PARTS,) + weights[2].shape[1:], bf16), pltpu.VMEM(weights[2].shape, bf16),
        pltpu.VMEM(params.shape, f32), rows(bf16), rows(bf16), rows(f32), rows(f32), rows(f32),
        pltpu.VMEM((length, LANES), f32), pltpu.VMEM((span, width), f32),
        pltpu.VMEM((SUBLANES, span - SUBLANES, width), f32), rows(f32), rows(bf16),
    ]
    return stage_call(
        forward_kernel, scratch, info, (incoming, frames, *weights, params), outs, buffers,
        taps, length, width, stage_cost(length, width), (3 + IN_PARTS, 8),
    )


def backward_stage(info, incoming, cotangent, weights, params, saved, buffers, taps):
    micro, length, width = cotangent.shape
    f32, bf16 = jnp.float32, jnp.bfloat16
    shape = jax.ShapeDtypeStruct
    outs = [
        shape((length, width), bf16), shape((micro, length, width), bf16),
        shape((micro, length, 2 * width), bf16), shape((micro, length, width), bf16),
        shape((micro, 2 * SUBLANES, width), f32), shape((micro, length, width), f32),
    ]
    rows = functools.partial(pltpu.VMEM, (length, width))
    span = length + 2 * MARGIN
    lifted = pltpu.VMEM((SUBLANES, span - SUBLANES, width), f32)
    scratch = [
        rows(bf16), pltpu.VMEM((IN_PARTS,) + weights[2].shape[1:], bf16), pltpu.VMEM(weights[2].shape, bf16),
        pltpu.VMEM(params.shape, f32), rows(bf16), rows(f32), rows(f32), rows(f32),
        pltpu.VMEM((length, LANES), f32), pltpu.VMEM((span, width), f32), lifted, rows(f32),
        pltpu.VMEM((length, 2 * width), bf16), pltpu.VMEM((2 * SUBLANES, width), f32),
        rows(bf16),
    ]
    return stage_call(
        backward_kernel, scratch, info, (incoming, cotangent, *weights, params) + tuple(saved),
        outs, buffers, taps, length, width, stage_cost(length, width), (8 + IN_PARTS, 6),
    )


def send_active(x, senders, by):
    pairs = [(s, s + by) for s in senders if 0 <= s + by < lax.axis_size("section")]
    return lax.ppermute(x, "section", pairs)


def local(frames, cotangent, lengths, w_in, w_out, gain_pre, gain_mid, w_depth):
    sections = lax.axis_size("section")
    section_index = lax.axis_index("section")
    micro_count = frames.shape[0]
    frames_len = frames.shape[2]
    model_width = frames.shape[3]
    slots = micro_count + SKEW * (sections - 1)
    scale = 1.0 / math.sqrt(
        micro_count * frames_len * lax.axis_size("fsdp") * lax.axis_size("batch")
    )
    weights = gather_weights(w_in[0], w_out[0])
    taps = w_depth.shape[1]
    params = jnp.concatenate(
        [
            w_depth[0],
            jnp.zeros((GAIN_A - taps, model_width), jnp.float32),
            gain_pre,
            jnp.zeros((GAIN_B - GAIN_A - 1, model_width), jnp.float32),
            gain_mid,
            jnp.zeros((PARAM_ROWS - GAIN_B - 1, model_width), jnp.float32),
        ],
        axis=0,
    )
    frame_rows = frames.reshape(micro_count, frames_len, model_width)
    cotangent_rows = cotangent.reshape(micro_count, frames_len, model_width)

    def info_table(place):
        micro_index = jnp.arange(slots, dtype=jnp.int32) - SKEW * place
        active = (micro_index >= 0) & (micro_index < micro_count)
        slot = jnp.clip(micro_index, 0, micro_count - 1)
        first = jnp.broadcast_to(place == 0, active.shape)
        valid = jnp.take(lengths[:, 0], slot)
        return jnp.stack([slot, active.astype(jnp.int32), first.astype(jnp.int32), valid], axis=1)

    def active_at(slot, flipped):
        places = [p for p in range(sections) if 0 <= slot - SKEW * p < micro_count]
        return [sections - 1 - p for p in places] if flipped else places

    blank = jnp.zeros((frames_len, model_width), jnp.bfloat16)
    pending = [blank] * SKEW
    table = info_table(section_index)
    saved = None
    for slot in range(slots):
        outgoing, *saved = forward_stage(
            table[slot], pending.pop(0), frame_rows, weights, params, saved, taps
        )
        pending.append(send_active(outgoing, active_at(slot, False), 1))
    x_all, proj_all, swish_all, value_all, gate_all, mid_all, inv_all = saved
    kept = (x_all, value_all, gate_all, mid_all, inv_all)
    pending = [blank] * SKEW
    table = info_table(sections - 1 - section_index)
    grads = None
    for slot in range(slots):
        outgoing, *grads = backward_stage(
            table[slot], pending.pop(0), cotangent_rows, weights, params, kept,
            grads, taps,
        )
        pending.append(send_active(outgoing, active_at(slot, True), -1))
    input_all, grad_all, up_all, small_all, conv_all = grads
    total_rows = micro_count * frames_len
    width = weights[2].shape[2]
    quarters = weights[0].shape[0]
    proj_rows = proj_all.reshape(total_rows, model_width)
    grad_rows = grad_all.reshape(total_rows, 2 * model_width)
    swish_rows = swish_all.reshape(total_rows, model_width)
    upstream_rows = up_all.reshape(total_rows, model_width)

    def term(left, right):
        return lax.dot_general(
            left, right, (((0,), (0,)), ((), ())), preferred_element_type=jnp.float32
        ).astype(jnp.bfloat16)

    def terms(left, right, parts):
        return jnp.stack(
            [term(left, right[:, part * width : (part + 1) * width]) for part in parts]
        )

    shared_terms = terms(proj_rows, grad_rows, range(quarters))
    rest_terms = terms(proj_rows, grad_rows, range(quarters, IN_PARTS))
    out_terms = terms(swish_rows, upstream_rows, range(weights[2].shape[0]))
    small_rows = jnp.sum(small_all, axis=0)
    tap_rows = taps_sums(lengths[:, 0], conv_all, value_all, gate_all, taps)
    small = jnp.concatenate(
        [
            small_rows[SMALL_A : SMALL_A + 1],
            small_rows[SMALL_B : SMALL_B + 1],
            tap_rows[:taps],
        ],
        axis=0,
    )
    grad_in, grad_out, small_total = reduce_weights(
        shared_terms, rest_terms, out_terms, small, scale
    )
    input_grads = input_all.reshape(1, micro_count, 1, frames_len, model_width)
    return (
        input_grads,
        grad_in[None],
        grad_out[None],
        small_total[0:1],
        small_total[1:2],
        small_total[2:][None],
    )


def solution(mesh):
    in_specs = (
        P(None, ("fsdp", "batch"), None, None),
        P(None, ("fsdp", "batch"), None, None),
        P(None, ("fsdp", "batch")),
        P("section", "fsdp", None),
        P("section", "fsdp", None),
        P("section", None),
        P("section", None),
        P("section", None, None),
    )
    out_specs = (
        P("section", None, ("fsdp", "batch"), None, None),
        P("section", "fsdp", None),
        P("section", "fsdp", None),
        P("section", None),
        P("section", None),
        P("section", None, None),
    )
    return jax.shard_map(local, mesh=mesh, in_specs=in_specs, out_specs=out_specs, check_vma=False)
```

```python
import functools
import math

import jax
import jax.numpy as jnp
from jax import lax
from jax.experimental import pallas as pl
from jax.experimental.pallas import tpu as pltpu
from jax.sharding import PartitionSpec as P

epsilon = 1e-05
LANES = 128
SUBLANES = 8
MARGIN = 16
GAIN_A = 32
GAIN_B = 40
PARAM_ROWS = 48
SKEW = 2
IN_PARTS = 6
SMALL_A = 0
SMALL_B = 8
LARGEST = 3.0e38
VMEM_LIMIT = 64 * 1024 * 1024 - 64 * 1024
PAIR = 2


def rotate(x, axis, by):
    peers = lax.axis_size(axis)
    return lax.ppermute(x, axis, [(i, (i + by) % peers) for i in range(peers)])


def swap_bit(x, bit):
    peers = lax.axis_size("fsdp")
    return lax.ppermute(x, "fsdp", [(i, i ^ bit) for i in range(peers)])


def ring_position():
    index = lax.axis_index("fsdp")
    return index // PAIR, index % PAIR


def pick(stacked, index, axis=0):
    return lax.dynamic_index_in_dim(stacked, index, axis, keepdims=False)


def after(x):
    value = jnp.abs(x.reshape(-1)[0].astype(jnp.float32))
    return jnp.where(value <= LARGEST, 0, 1).astype(jnp.int32)


def column_parts(x, width):
    return [x[:, start : start + width] for start in range(0, x.shape[1], width)]


def ring_gather(payload, place, far_split):
    ring = lax.axis_size("fsdp") // PAIR
    half = ring // 2
    up, down = payload, payload
    for hop in range(1, half):
        up = rotate(up, "fsdp", PAIR)
        down = rotate(down, "fsdp", -PAIR)
        place(up, ring - hop)
        place(down, hop)
    far_up = rotate(up[:far_split], "fsdp", PAIR)
    far_down = rotate(down[far_split:], "fsdp", -PAIR)
    place(jnp.concatenate([far_up, far_down], axis=0), half)


def gather_weights(w_in, w_out):
    quarters = lax.axis_size("batch")
    ring = lax.axis_size("fsdp") // PAIR
    at, side = ring_position()
    rows, width = w_in.shape[0], w_in.shape[1] // IN_PARTS
    out_parts = w_out.shape[1] // width
    rest = IN_PARTS - quarters
    mine = lax.dynamic_slice_in_dim(w_in, lax.axis_index("batch") * width, width, 1)
    first = jnp.stack([mine] + column_parts(w_in, width)[quarters:])
    other = swap_bit(first, 1)
    both = jnp.where(side == 0, jnp.stack([first, other], 1), jnp.stack([other, first], 1))
    shared = jnp.zeros((ring, PAIR, rows, width), w_in.dtype)
    whole = jnp.zeros((rest, ring, PAIR, rows, width), w_in.dtype)
    out = jnp.zeros((out_parts, ring, PAIR, rows, width), w_in.dtype)

    def place_shared(piece, offset):
        nonlocal shared
        spot = ((at + offset) % ring, 0, 0, 0)
        shared = lax.dynamic_update_slice(shared, piece[None], spot)

    def place_out(piece, offset, where):
        nonlocal out
        spot = (0, (at + offset) % ring, where, 0, 0)
        out = lax.dynamic_update_slice(out, piece[:, None, None], spot)

    def place_rest(piece, offset):
        nonlocal whole
        pair = piece[: rest * PAIR].reshape(rest, 1, PAIR, rows, width)
        whole = lax.dynamic_update_slice(whole, pair, (0, (at + offset) % ring, 0, 0, 0))
        own = piece[rest * PAIR :]
        place_out(own, offset, side)
        place_out(swap_bit(own, 1), offset, 1 - side)

    place_shared(both[0], 0)
    ring_gather(both[0], place_shared, 1)
    payload = jnp.concatenate(
        [both[1:].reshape(rest * PAIR, rows, width), jnp.stack(column_parts(w_out, width))]
    )
    place_rest(payload, 0)
    ring_gather(payload, place_rest, (rest * PAIR + out_parts) // 2)
    depth = ring * PAIR * rows
    shared = lax.all_gather(shared.reshape(depth, width), "batch", axis=0, tiled=False)
    return shared, whole.reshape(rest, depth, width), out.reshape(out_parts, depth, width)


def ring_scatter(term_at, far_split, prepare=lambda hop, tie: None):
    ring = lax.axis_size("fsdp") // PAIR
    half = ring // 2
    far = term_at(half)
    kind = far.dtype
    prepare(half - 1, far)
    up = rotate(far[:far_split], "fsdp", PAIR).astype(jnp.float32)
    down = rotate(far[far_split:], "fsdp", -PAIR).astype(jnp.float32)
    for hop in range(half - 1, 0, -1):
        mine_up = term_at(hop).astype(jnp.float32)
        mine_down = term_at(ring - hop).astype(jnp.float32)
        if hop == half - 1:
            up = jnp.concatenate([mine_up[:far_split] + up, mine_up[far_split:]])
            down = jnp.concatenate([mine_down[:far_split], mine_down[far_split:] + down])
        else:
            up = mine_up + up
            down = mine_down + down
        up = up.astype(kind)
        down = down.astype(kind)
        prepare(hop - 1, up)
        up = rotate(up, "fsdp", PAIR).astype(jnp.float32)
        down = rotate(down, "fsdp", -PAIR).astype(jnp.float32)
    return term_at(0).astype(jnp.float32) + up + down


def keep_side(total, kind):
    side = lax.axis_index("fsdp") % PAIR
    mine = jnp.where(side == 0, total[:, 0], total[:, 1])
    theirs = jnp.where(side == 0, total[:, 1], total[:, 0])
    return mine + swap_bit(theirs.astype(kind), 1).astype(jnp.float32)


def batch_copies(x):
    return x, rotate(x, "batch", 1), rotate(x, "batch", 2), rotate(x, "batch", 3)


def batch_order(copies):
    quarters = len(copies)
    here = lax.axis_index("batch")
    stacked = jnp.stack(copies)
    return [pick(stacked, (here + quarters - part) % quarters) for part in range(quarters)]


def sum_batch(x):
    own, left, far, right = (part.astype(jnp.float32) for part in batch_copies(x))
    return (own + far) + (left + right)


def small_steps(small):
    quarters = lax.axis_size("batch")
    here = lax.axis_index("batch")
    width = small.shape[1] // quarters
    pieces = jnp.stack(column_parts(small, width))
    tie = yield None
    mine = pick(pieces, here)
    for by in range(1, quarters):
        mine = mine + rotate(pick(pieces, (here + by) % quarters + tie), "batch", by)
    bit = 1
    while bit < lax.axis_size("fsdp"):
        tie = yield None
        mine = mine + swap_bit(mine + tie.astype(jnp.float32), bit)
        bit *= 2
    tie = yield None
    mine = mine + tie.astype(jnp.float32)
    yield jnp.concatenate(batch_order(batch_copies(mine)), axis=1)


def reduce_weights(shared, rest, out, small, scale):
    ring = lax.axis_size("fsdp") // PAIR
    at, side = ring_position()
    kind = shared.dtype
    quarters, depth, width = shared.shape
    rows = depth // (ring * PAIR)
    split = (ring, PAIR, rows, width)
    shared_sum = lax.psum_scatter(shared, "batch", scatter_dimension=0, tiled=False).reshape(split)
    rest_pairs = rest.reshape((-1,) + split)
    out_pairs = out.reshape((-1,) + split)
    rest_parts, out_parts = rest_pairs.shape[0], out_pairs.shape[0]
    steps = small_steps(small)
    next(steps)
    given = {}

    def out_for(offset, where):
        spot = pick(out_pairs, (at + offset) % ring, 1)
        return pick(spot, where, 1)

    def exchange(offsets, tie):
        theirs = jnp.concatenate([out_for(offset + tie, 1 - side) for offset in offsets])
        arrived = swap_bit(theirs, 1)
        for number, offset in enumerate(offsets):
            given[offset] = arrived[number * out_parts : (number + 1) * out_parts]

    def main_term(offset):
        pair = pick(rest_pairs, (at + offset) % ring, 1).reshape(-1, rows, width)
        extra = given[offset].astype(jnp.float32)
        own = (out_for(offset, side).astype(jnp.float32) + extra).astype(kind)
        return jnp.concatenate([pair, own])

    def prepare(hop, ready):
        tie = after(ready)
        if hop == 0:
            tie = tie + after(shared_sum)
        exchange([hop, ring - hop] if hop else [0], tie)
        steps.send(tie)

    late = []

    def note(hop, ready):
        if hop == 1:
            late.append(after(ready))

    exchange([ring // 2], 0)
    steps.send(jnp.int32(0))
    total = ring_scatter(main_term, (rest_parts * PAIR + out_parts) // 2, prepare)
    small_total = scale * steps.send(after(total))
    rest_share = keep_side(
        total[: rest_parts * PAIR].reshape(rest_parts, PAIR, rows, width), kind
    )
    shared_total = ring_scatter(
        lambda offset: pick(shared_sum, (at + offset) % ring), 1, note
    )
    share = jnp.concatenate([rest_share, total[rest_parts * PAIR :]])
    share = sum_batch((share + late[0].astype(jnp.float32)).astype(kind))
    shared_share = keep_side(shared_total[None], kind)[0].astype(kind)
    in_parts = [part.astype(jnp.float32) for part in batch_order(batch_copies(shared_share))]
    grad_in = jnp.concatenate(in_parts + [share[part] for part in range(rest_parts)], axis=1)
    grad_out = jnp.concatenate([share[rest_parts + part] for part in range(out_parts)], axis=1)
    return scale * grad_in, scale * grad_out, small_total


def layer_stats(values):
    mean_value = jnp.mean(values, axis=-1, keepdims=True)
    centred = values - mean_value
    inv_scale = lax.rsqrt(jnp.mean(centred * centred, axis=-1, keepdims=True) + epsilon)
    return centred * inv_scale, inv_scale


def norm_grad(upstream, normed, inv_scale):
    return (
        upstream
        - jnp.mean(upstream, axis=-1, keepdims=True)
        - normed * jnp.mean(upstream * normed, axis=-1, keepdims=True)
    ) * inv_scale


def rows_by(left, right):
    return jnp.dot(left, right, preferred_element_type=jnp.float32)


def rows_back(left, right):
    return lax.dot_general(
        left, right, (((1,), (1,)), ((), ())), preferred_element_type=jnp.float32
    )


def write_shifts(shifts, padded):
    span = shifts.shape[1]

    def shift(lanes):
        for by in range(SUBLANES):
            shifts[by, :, lanes] = padded[pl.ds(by, span), lanes]

    each_lane_block(padded.shape[1], shift)


def clear_margins(padded, length):
    zeros = jnp.zeros((MARGIN, padded.shape[1]), jnp.float32)
    padded[pl.ds(0, MARGIN), :] = zeros
    padded[pl.ds(MARGIN + length, MARGIN), :] = zeros


def each_block(width, size, body):
    def step(block, carry):
        body(block, pl.ds(pl.multiple_of(block * size, size), size))
        return carry

    lax.fori_loop(0, width // size, step, 0)


def each_lane_block(width, body):
    each_block(width, LANES, lambda block, lanes: body(lanes))


def shifted(shifts, offset, length, lanes):
    start = offset // SUBLANES * SUBLANES
    return shifts[offset % SUBLANES, pl.ds(start, length), lanes]


def part_copy(source, index, target, part, sems, base):
    return pltpu.make_async_copy(source.at[index], target.at[part], sems.at[base + part])


def start_parts(shared, rest, target, sems, base):
    for part in range(shared.shape[0]):
        part_copy(shared, part, target, part, sems, base).start()
    for part in range(rest.shape[0]):
        part_copy(rest, part, target, shared.shape[0] + part, sems, base).start()


def forward_kernel(
    info, incoming, frames, w_shared, w_rest, w_out, params, *refs, taps, length, width, aliased
):
    refs = refs[aliased:]
    outgoing, x_all, proj_all, swish_all, value_all, gate_all, mid_all, inv_all = refs[:8]
    (
        x_v, w_in_v, w_out_v, params_v, proj_v, swish_v, value_v, gate_v, mid_v, inv_v,
        padded, shifts, conv_v, out_v, in_sems, out_sems,
    ) = refs[8:]
    slot, active, first, valid = info[0], info[1], info[2], info[3]
    parts = w_in_v.shape[0]
    half = taps // 2

    @pl.when(active == 1)
    def run():
        x_copy = pltpu.make_async_copy(incoming, x_v, in_sems.at[0])
        frame_copy = pltpu.make_async_copy(frames.at[slot], x_v, in_sems.at[0])

        @pl.when(first == 1)
        def from_frames():
            frame_copy.start()

        @pl.when(first == 0)
        def from_neighbour():
            x_copy.start()

        params_copy = pltpu.make_async_copy(params, params_v, in_sems.at[1])
        params_copy.start()
        start_parts(w_shared, w_rest, w_in_v, in_sems, 2)
        w_out_copy = pltpu.make_async_copy(w_out, w_out_v, in_sems.at[2 + parts])
        w_out_copy.start()
        saves = []

        def save(source, target):
            copy = pltpu.make_async_copy(source, target, out_sems.at[len(saves)])
            copy.start()
            saves.append(copy)

        clear_margins(padded, length)
        x_copy.wait()
        params_copy.wait()
        source = x_v[...].astype(jnp.float32)
        save(x_v, x_all.at[slot])
        normed_in, unused = layer_stats(source)
        proj_v[...] = (normed_in * params_v[pl.ds(GAIN_A, 1), :]).astype(jnp.bfloat16)
        save(proj_v, proj_all.at[slot])
        part_width = w_in_v.shape[2]

        def into_value(part, lanes):
            part_copy(w_shared, 0, w_in_v, part, in_sems, 2).wait()
            value_v[:, lanes] = rows_by(proj_v[...], w_in_v[part])

        def into_gate(block, lanes):
            part = block + parts // 2
            part_copy(w_shared, 0, w_in_v, part, in_sems, 2).wait()
            gate_v[:, lanes] = jax.nn.sigmoid(rows_by(proj_v[...], w_in_v[part]))

        each_block(width, part_width, into_value)
        each_block(width, part_width, into_gate)
        save(value_v, value_all.at[slot])
        save(gate_v, gate_all.at[slot])
        rows = lax.broadcasted_iota(jnp.int32, (length, width), 0)
        mask = (rows < valid).astype(jnp.float32)
        padded[pl.ds(MARGIN, length), :] = value_v[...] * gate_v[...] * mask
        write_shifts(shifts, padded)

        def convolve(lanes):
            total = jnp.zeros((length, LANES), jnp.float32)
            for tap in range(taps):
                weight = params_v[pl.ds(tap, 1), lanes]
                total = total + shifted(shifts, tap + MARGIN - half, length, lanes) * weight
            conv_v[:, lanes] = total

        each_lane_block(width, convolve)
        normed_mid, inv_mid = layer_stats(conv_v[...])
        mid_v[...] = normed_mid
        inv_v[...] = jnp.broadcast_to(inv_mid, inv_v.shape)
        save(mid_v, mid_all.at[slot])
        save(inv_v, inv_all.at[slot])
        scaled_mid = normed_mid * params_v[pl.ds(GAIN_B, 1), :]
        swish_v[...] = (scaled_mid * jax.nn.sigmoid(scaled_mid)).astype(jnp.bfloat16)
        save(swish_v, swish_all.at[slot])
        w_out_copy.wait()

        def into_out(block, lanes):
            source = x_v[:, lanes].astype(jnp.float32)
            out_v[:, lanes] = (source + rows_by(swish_v[...], w_out_v[block])).astype(jnp.bfloat16)

        each_block(width, part_width, into_out)
        save(out_v, outgoing)
        for copy in saves:
            copy.wait()


def backward_kernel(
    info, incoming, cotangent, w_shared, w_rest, w_out, params,
    x_all, value_all, gate_all, mid_all, inv_all, *refs, taps, length, width, aliased
):
    refs = refs[aliased:]
    outgoing, input_all, grad_all, up_all, small_all, conv_all = refs[:6]
    (
        u_v, w_in_v, w_out_v, params_v, x_v, value_v, gate_v, mid_v, inv_v,
        padded_grad, shifts_grad, conv_v, grad_v, small_v, out_v,
        in_sems, out_sems,
    ) = refs[6:]
    slot, active, first, valid = info[0], info[1], info[2], info[3]
    parts = w_in_v.shape[0]
    half = taps // 2

    @pl.when(active == 1)
    def run():
        u_copy = pltpu.make_async_copy(incoming, u_v, in_sems.at[0])
        given_copy = pltpu.make_async_copy(cotangent.at[slot], u_v, in_sems.at[0])

        @pl.when(first == 1)
        def from_cotangent():
            given_copy.start()

        @pl.when(first == 0)
        def from_neighbour():
            u_copy.start()

        w_out_copy = pltpu.make_async_copy(w_out, w_out_v, in_sems.at[1])
        w_out_copy.start()
        loads = []
        for number, (source, target) in enumerate((
            (params, params_v),
            (value_all.at[slot], value_v),
            (gate_all.at[slot], gate_v),
            (mid_all.at[slot], mid_v),
            (inv_all.at[slot], inv_v),
            (x_all.at[slot], x_v),
        )):
            copy = pltpu.make_async_copy(source, target, in_sems.at[2 + number])
            copy.start()
            loads.append(copy)
        start_parts(w_shared, w_rest, w_in_v, in_sems, 8)
        saves = []

        def save(source, target):
            copy = pltpu.make_async_copy(source, target, out_sems.at[len(saves)])
            copy.start()
            saves.append(copy)

        clear_margins(padded_grad, length)
        small_v[...] = jnp.zeros_like(small_v)
        for copy in loads:
            copy.wait()
        rows = lax.broadcasted_iota(jnp.int32, (length, width), 0)
        mask = (rows < valid).astype(jnp.float32)
        u_copy.wait()
        save(u_v, up_all.at[slot])
        w_out_copy.wait()
        part_width = w_in_v.shape[2]
        conv_v[...] = jnp.zeros_like(conv_v)

        def into_swish(block, lanes):
            conv_v[...] += rows_back(u_v[:, lanes], w_out_v[block])

        each_block(width, part_width, into_swish)
        swish_grad = conv_v[...]
        normed_mid = mid_v[...]
        gain_b = params_v[pl.ds(GAIN_B, 1), :]
        scaled_mid = normed_mid * gain_b
        sigmoid_mid = jax.nn.sigmoid(scaled_mid)
        scaled_grad = swish_grad * (
            sigmoid_mid + scaled_mid * sigmoid_mid * (1.0 - sigmoid_mid)
        )
        small_v[pl.ds(SMALL_B, 1), :] = jnp.sum(scaled_grad * normed_mid, axis=0, keepdims=True)
        conv_grad = norm_grad(scaled_grad * gain_b, normed_mid, inv_v[:, :1])
        padded_grad[pl.ds(MARGIN, length), :] = conv_grad
        save(padded_grad.at[pl.ds(MARGIN, length), :], conv_all.at[slot])
        write_shifts(shifts_grad, padded_grad)

        def convolve(lanes):
            total = jnp.zeros((length, LANES), jnp.float32)
            for tap in range(taps):
                weight = params_v[pl.ds(tap, 1), lanes]
                total = total + shifted(shifts_grad, MARGIN + half - tap, length, lanes) * weight
            conv_v[:, lanes] = total

        each_lane_block(width, convolve)

        gated_grad = conv_v[...] * mask
        glu_gate = gate_v[...]
        grad_v[:, :width] = (gated_grad * glu_gate).astype(jnp.bfloat16)
        grad_v[:, width:] = (
            gated_grad * value_v[...] * glu_gate * (1.0 - glu_gate)
        ).astype(jnp.bfloat16)
        save(grad_v, grad_all.at[slot])
        conv_v[...] = jnp.zeros_like(conv_v)

        def into_input(part, lanes):
            part_copy(w_shared, 0, w_in_v, part, in_sems, 8).wait()
            conv_v[...] += rows_back(grad_v[:, lanes], w_in_v[part])

        each_block(2 * width, part_width, into_input)
        input_side = conv_v[...]
        normed_in, inv_in = layer_stats(x_v[...].astype(jnp.float32))
        small_v[pl.ds(SMALL_A, 1), :] = jnp.sum(input_side * normed_in, axis=0, keepdims=True)
        save(small_v, small_all.at[slot])
        gain_a = params_v[pl.ds(GAIN_A, 1), :]
        out_v[...] = (
            u_v[...].astype(jnp.float32) + norm_grad(input_side * gain_a, normed_in, inv_in)
        ).astype(jnp.bfloat16)
        save(out_v, outgoing)
        save(out_v, input_all.at[slot])
        for copy in saves:
            copy.wait()


def taps_kernel(valid, grads, values, gates, out, padded, shifts, *, taps, length, width):
    micro = pl.program_id(0)

    @pl.when(micro == 0)
    def clear():
        out[...] = jnp.zeros_like(out)
        clear_margins(padded, length)

    rows = lax.broadcasted_iota(jnp.int32, (length, width), 0)
    mask = (rows < valid[micro]).astype(jnp.float32)
    padded[pl.ds(MARGIN, length), :] = values[0] * gates[0] * mask
    write_shifts(shifts, padded)

    def correlate(lanes):
        given = grads[0, :, lanes]
        for tap in range(taps):
            product = given * shifted(shifts, tap + MARGIN - taps // 2, length, lanes)
            out[pl.ds(tap, 1), lanes] += jnp.sum(product, axis=0, keepdims=True)

    each_lane_block(width, correlate)


def taps_sums(valid, grads, values, gates, taps):
    micro, length, width = grads.shape
    span = length + 2 * MARGIN
    block = pl.BlockSpec((1, length, width), lambda index, valid: (index, 0, 0))
    return pl.pallas_call(
        functools.partial(taps_kernel, taps=taps, length=length, width=width),
        grid_spec=pltpu.PrefetchScalarGridSpec(
            num_scalar_prefetch=1,
            grid=(micro,),
            in_specs=[block] * 3,
            out_specs=pl.BlockSpec((GAIN_A, width), lambda index, valid: (0, 0)),
            scratch_shapes=[
                pltpu.VMEM((span, width), jnp.float32),
                pltpu.VMEM((SUBLANES, span - SUBLANES, width), jnp.float32),
            ],
        ),
        out_shape=jax.ShapeDtypeStruct((GAIN_A, width), jnp.float32),
        compiler_params=pltpu.CompilerParams(vmem_limit_bytes=32 * 1024 * 1024),
        cost_estimate=pl.CostEstimate(
            flops=2 * taps * micro * length * width,
            transcendentals=0,
            bytes_accessed=12 * micro * length * width,
        ),
    )(valid, grads, values, gates)


def stage_call(kernel, scratch, info, inputs, out_shapes, buffers, taps, length, width, cost, sems):
    anywhere = pl.BlockSpec(memory_space=pl.ANY)
    aliases = {}
    operands = list(inputs)
    aliased = 0
    if buffers is not None:
        aliased = len(buffers)
        aliases = {1 + len(inputs) + number: 1 + number for number in range(aliased)}
        operands += list(buffers)
    in_sems, out_sems = sems
    return pl.pallas_call(
        functools.partial(kernel, taps=taps, length=length, width=width, aliased=aliased),
        grid_spec=pltpu.PrefetchScalarGridSpec(
            num_scalar_prefetch=1,
            grid=(),
            in_specs=[anywhere] * len(operands),
            out_specs=[anywhere] * len(out_shapes),
            scratch_shapes=list(scratch)
            + [pltpu.SemaphoreType.DMA((in_sems,)), pltpu.SemaphoreType.DMA((out_sems,))],
        ),
        out_shape=out_shapes,
        input_output_aliases=aliases,
        compiler_params=pltpu.CompilerParams(vmem_limit_bytes=VMEM_LIMIT),
        cost_estimate=cost,
    )(info, *operands)


def stage_cost(length, width):
    return pl.CostEstimate(
        flops=6 * length * width * width,
        transcendentals=2 * length * width,
        bytes_accessed=6 * width * width,
    )


def forward_stage(info, incoming, frames, weights, params, buffers, taps):
    micro, length, width = frames.shape
    f32, bf16 = jnp.float32, jnp.bfloat16
    shape = jax.ShapeDtypeStruct
    outs = [shape((length, width), bf16)] + [
        shape((micro, length, width), dtype) for dtype in (bf16, bf16, bf16, f32, f32, f32)
    ] + [shape((micro, length, LANES), f32)]
    rows = functools.partial(pltpu.VMEM, (length, width))
    span = length + 2 * MARGIN
    scratch = [
        rows(bf16), pltpu.VMEM((IN_PARTS,) + weights[2].shape[1:], bf16), pltpu.VMEM(weights[2].shape, bf16),
        pltpu.VMEM(params.shape, f32), rows(bf16), rows(bf16), rows(f32), rows(f32), rows(f32),
        pltpu.VMEM((length, LANES), f32), pltpu.VMEM((span, width), f32),
        pltpu.VMEM((SUBLANES, span - SUBLANES, width), f32), rows(f32), rows(bf16),
    ]
    return stage_call(
        forward_kernel, scratch, info, (incoming, frames, *weights, params), outs, buffers,
        taps, length, width, stage_cost(length, width), (3 + IN_PARTS, 8),
    )


def backward_stage(info, incoming, cotangent, weights, params, saved, buffers, taps):
    micro, length, width = cotangent.shape
    f32, bf16 = jnp.float32, jnp.bfloat16
    shape = jax.ShapeDtypeStruct
    outs = [
        shape((length, width), bf16), shape((micro, length, width), bf16),
        shape((micro, length, 2 * width), bf16), shape((micro, length, width), bf16),
        shape((micro, 2 * SUBLANES, width), f32), shape((micro, length, width), f32),
    ]
    rows = functools.partial(pltpu.VMEM, (length, width))
    span = length + 2 * MARGIN
    lifted = pltpu.VMEM((SUBLANES, span - SUBLANES, width), f32)
    scratch = [
        rows(bf16), pltpu.VMEM((IN_PARTS,) + weights[2].shape[1:], bf16), pltpu.VMEM(weights[2].shape, bf16),
        pltpu.VMEM(params.shape, f32), rows(bf16), rows(f32), rows(f32), rows(f32),
        pltpu.VMEM((length, LANES), f32), pltpu.VMEM((span, width), f32), lifted, rows(f32),
        pltpu.VMEM((length, 2 * width), bf16), pltpu.VMEM((2 * SUBLANES, width), f32),
        rows(bf16),
    ]
    return stage_call(
        backward_kernel, scratch, info, (incoming, cotangent, *weights, params) + tuple(saved),
        outs, buffers, taps, length, width, stage_cost(length, width), (8 + IN_PARTS, 6),
    )


def send_active(x, senders, by):
    pairs = [(s, s + by) for s in senders if 0 <= s + by < lax.axis_size("section")]
    return lax.ppermute(x, "section", pairs)


def local(frames, cotangent, lengths, w_in, w_out, gain_pre, gain_mid, w_depth):
    sections = lax.axis_size("section")
    section_index = lax.axis_index("section")
    micro_count = frames.shape[0]
    frames_len = frames.shape[2]
    model_width = frames.shape[3]
    slots = micro_count + SKEW * (sections - 1)
    scale = 1.0 / math.sqrt(
        micro_count * frames_len * lax.axis_size("fsdp") * lax.axis_size("batch")
    )
    weights = gather_weights(w_in[0], w_out[0])
    taps = w_depth.shape[1]
    params = jnp.concatenate(
        [
            w_depth[0],
            jnp.zeros((GAIN_A - taps, model_width), jnp.float32),
            gain_pre,
            jnp.zeros((GAIN_B - GAIN_A - 1, model_width), jnp.float32),
            gain_mid,
            jnp.zeros((PARAM_ROWS - GAIN_B - 1, model_width), jnp.float32),
        ],
        axis=0,
    )
    frame_rows = frames.reshape(micro_count, frames_len, model_width)
    cotangent_rows = cotangent.reshape(micro_count, frames_len, model_width)

    def info_table(place):
        micro_index = jnp.arange(slots, dtype=jnp.int32) - SKEW * place
        active = (micro_index >= 0) & (micro_index < micro_count)
        slot = jnp.clip(micro_index, 0, micro_count - 1)
        first = jnp.broadcast_to(place == 0, active.shape)
        valid = jnp.take(lengths[:, 0], slot)
        return jnp.stack([slot, active.astype(jnp.int32), first.astype(jnp.int32), valid], axis=1)

    def active_at(slot, flipped):
        places = [p for p in range(sections) if 0 <= slot - SKEW * p < micro_count]
        return [sections - 1 - p for p in places] if flipped else places

    blank = jnp.zeros((frames_len, model_width), jnp.bfloat16)
    pending = [blank] * SKEW
    table = info_table(section_index)
    saved = None
    for slot in range(slots):
        outgoing, *saved = forward_stage(
            table[slot], pending.pop(0), frame_rows, weights, params, saved, taps
        )
        pending.append(send_active(outgoing, active_at(slot, False), 1))
    x_all, proj_all, swish_all, value_all, gate_all, mid_all, inv_all = saved
    kept = (x_all, value_all, gate_all, mid_all, inv_all)
    pending = [blank] * SKEW
    table = info_table(sections - 1 - section_index)
    grads = None
    for slot in range(slots):
        outgoing, *grads = backward_stage(
            table[slot], pending.pop(0), cotangent_rows, weights, params, kept,
            grads, taps,
        )
        pending.append(send_active(outgoing, active_at(slot, True), -1))
    input_all, grad_all, up_all, small_all, conv_all = grads
    total_rows = micro_count * frames_len
    width = weights[2].shape[2]
    quarters = weights[0].shape[0]
    proj_rows = proj_all.reshape(total_rows, model_width)
    grad_rows = grad_all.reshape(total_rows, 2 * model_width)
    swish_rows = swish_all.reshape(total_rows, model_width)
    upstream_rows = up_all.reshape(total_rows, model_width)

    def term(left, right):
        return lax.dot_general(
            left, right, (((0,), (0,)), ((), ())), preferred_element_type=jnp.float32
        ).astype(jnp.bfloat16)

    def terms(left, right, parts):
        return jnp.stack(
            [term(left, right[:, part * width : (part + 1) * width]) for part in parts]
        )

    shared_terms = terms(proj_rows, grad_rows, range(quarters))
    rest_terms = terms(proj_rows, grad_rows, range(quarters, IN_PARTS))
    out_terms = terms(swish_rows, upstream_rows, range(weights[2].shape[0]))
    small_rows = jnp.sum(small_all, axis=0)
    tap_rows = taps_sums(lengths[:, 0], conv_all, value_all, gate_all, taps)
    small = jnp.concatenate(
        [
            small_rows[SMALL_A : SMALL_A + 1],
            small_rows[SMALL_B : SMALL_B + 1],
            tap_rows[:taps],
        ],
        axis=0,
    )
    grad_in, grad_out, small_total = reduce_weights(
        shared_terms, rest_terms, out_terms, small, scale
    )
    input_grads = input_all.reshape(1, micro_count, 1, frames_len, model_width)
    return (
        input_grads,
        grad_in[None],
        grad_out[None],
        small_total[0:1],
        small_total[1:2],
        small_total[2:][None],
    )


def solution(mesh):
    in_specs = (
        P(None, ("fsdp", "batch"), None, None),
        P(None, ("fsdp", "batch"), None, None),
        P(None, ("fsdp", "batch")),
        P("section", "fsdp", None),
        P("section", "fsdp", None),
        P("section", None),
        P("section", None),
        P("section", None, None),
    )
    out_specs = (
        P("section", None, ("fsdp", "batch"), None, None),
        P("section", "fsdp", None),
        P("section", "fsdp", None),
        P("section", None),
        P("section", None),
        P("section", None, None),
    )
    return jax.shard_map(local, mesh=mesh, in_specs=in_specs, out_specs=out_specs, check_vma=False)
```

```python
import functools
import math

import jax
import jax.numpy as jnp
from jax import lax
from jax.experimental import pallas as pl
from jax.experimental.pallas import tpu as pltpu
from jax.sharding import PartitionSpec as P

epsilon = 1e-05
LANES = 128
SUBLANES = 8
MARGIN = 16
GAIN_A = 32
GAIN_B = 40
PARAM_ROWS = 48
SKEW = 2
IN_PARTS = 6
SMALL_A = 0
SMALL_B = 8
LARGEST = 3.0e38
VMEM_LIMIT = 64 * 1024 * 1024 - 64 * 1024
PAIR = 2


def rotate(x, axis, by):
    peers = lax.axis_size(axis)
    return lax.ppermute(x, axis, [(i, (i + by) % peers) for i in range(peers)])


def swap_bit(x, bit):
    peers = lax.axis_size("fsdp")
    return lax.ppermute(x, "fsdp", [(i, i ^ bit) for i in range(peers)])


def ring_position():
    index = lax.axis_index("fsdp")
    return index // PAIR, index % PAIR


def pick(stacked, index, axis=0):
    return lax.dynamic_index_in_dim(stacked, index, axis, keepdims=False)


def after(x):
    value = jnp.abs(x.reshape(-1)[0].astype(jnp.float32))
    return jnp.where(value <= LARGEST, 0, 1).astype(jnp.int32)


def column_parts(x, width):
    return [x[:, start : start + width] for start in range(0, x.shape[1], width)]


def ring_gather(payload, place, far_split):
    ring = lax.axis_size("fsdp") // PAIR
    half = ring // 2
    up, down = payload, payload
    for hop in range(1, half):
        up = rotate(up, "fsdp", PAIR)
        down = rotate(down, "fsdp", -PAIR)
        place(up, ring - hop)
        place(down, hop)
    far_up = rotate(up[:far_split], "fsdp", PAIR)
    far_down = rotate(down[far_split:], "fsdp", -PAIR)
    place(jnp.concatenate([far_up, far_down], axis=0), half)


def gather_weights(w_in, w_out):
    quarters = lax.axis_size("batch")
    ring = lax.axis_size("fsdp") // PAIR
    at, side = ring_position()
    rows, width = w_in.shape[0], w_in.shape[1] // IN_PARTS
    out_parts = w_out.shape[1] // width
    rest = IN_PARTS - quarters
    mine = lax.dynamic_slice_in_dim(w_in, lax.axis_index("batch") * width, width, 1)
    first = jnp.stack([mine] + column_parts(w_in, width)[quarters:])
    other = swap_bit(first, 1)
    both = jnp.where(side == 0, jnp.stack([first, other], 1), jnp.stack([other, first], 1))
    shared = jnp.zeros((ring, PAIR, rows, width), w_in.dtype)
    whole = jnp.zeros((rest, ring, PAIR, rows, width), w_in.dtype)
    out = jnp.zeros((out_parts, ring, PAIR, rows, width), w_in.dtype)

    def place_shared(piece, offset):
        nonlocal shared
        spot = ((at + offset) % ring, 0, 0, 0)
        shared = lax.dynamic_update_slice(shared, piece[None], spot)

    def place_out(piece, offset, where):
        nonlocal out
        spot = (0, (at + offset) % ring, where, 0, 0)
        out = lax.dynamic_update_slice(out, piece[:, None, None], spot)

    def place_rest(piece, offset):
        nonlocal whole
        pair = piece[: rest * PAIR].reshape(rest, 1, PAIR, rows, width)
        whole = lax.dynamic_update_slice(whole, pair, (0, (at + offset) % ring, 0, 0, 0))
        own = piece[rest * PAIR :]
        place_out(own, offset, side)
        place_out(swap_bit(own, 1), offset, 1 - side)

    place_shared(both[0], 0)
    ring_gather(both[0], place_shared, 1)
    payload = jnp.concatenate(
        [both[1:].reshape(rest * PAIR, rows, width), jnp.stack(column_parts(w_out, width))]
    )
    place_rest(payload, 0)
    ring_gather(payload, place_rest, (rest * PAIR + out_parts) // 2)
    depth = ring * PAIR * rows
    shared = lax.all_gather(shared.reshape(depth, width), "batch", axis=0, tiled=False)
    return shared, whole.reshape(rest, depth, width), out.reshape(out_parts, depth, width)


def ring_scatter(term_at, far_split, prepare=lambda hop, tie: None):
    ring = lax.axis_size("fsdp") // PAIR
    half = ring // 2
    far = term_at(half)
    kind = far.dtype
    prepare(half - 1, far)
    up = rotate(far[:far_split], "fsdp", PAIR).astype(jnp.float32)
    down = rotate(far[far_split:], "fsdp", -PAIR).astype(jnp.float32)
    for hop in range(half - 1, 0, -1):
        mine_up = term_at(hop).astype(jnp.float32)
        mine_down = term_at(ring - hop).astype(jnp.float32)
        if hop == half - 1:
            up = jnp.concatenate([mine_up[:far_split] + up, mine_up[far_split:]])
            down = jnp.concatenate([mine_down[:far_split], mine_down[far_split:] + down])
        else:
            up = mine_up + up
            down = mine_down + down
        up = up.astype(kind)
        down = down.astype(kind)
        prepare(hop - 1, up)
        up = rotate(up, "fsdp", PAIR).astype(jnp.float32)
        down = rotate(down, "fsdp", -PAIR).astype(jnp.float32)
    return term_at(0).astype(jnp.float32) + up + down


def keep_side(total, kind):
    side = lax.axis_index("fsdp") % PAIR
    mine = jnp.where(side == 0, total[:, 0], total[:, 1])
    theirs = jnp.where(side == 0, total[:, 1], total[:, 0])
    return mine + swap_bit(theirs.astype(kind), 1).astype(jnp.float32)


def batch_copies(x):
    return x, rotate(x, "batch", 1), rotate(x, "batch", 2), rotate(x, "batch", 3)


def batch_order(copies):
    quarters = len(copies)
    here = lax.axis_index("batch")
    stacked = jnp.stack(copies)
    return [pick(stacked, (here + quarters - part) % quarters) for part in range(quarters)]


def sum_batch(x):
    own, left, far, right = (part.astype(jnp.float32) for part in batch_copies(x))
    return (own + far) + (left + right)


def small_steps(small):
    quarters = lax.axis_size("batch")
    here = lax.axis_index("batch")
    width = small.shape[1] // quarters
    pieces = jnp.stack(column_parts(small, width))
    tie = yield None
    mine = pick(pieces, here)
    for by in range(1, quarters):
        mine = mine + rotate(pick(pieces, (here + by) % quarters + tie), "batch", by)
    bit = 1
    while bit < lax.axis_size("fsdp"):
        tie = yield None
        mine = mine + swap_bit(mine + tie.astype(jnp.float32), bit)
        bit *= 2
    tie = yield None
    mine = mine + tie.astype(jnp.float32)
    yield jnp.concatenate(batch_order(batch_copies(mine)), axis=1)


def reduce_weights(shared, rest, out, small, scale):
    ring = lax.axis_size("fsdp") // PAIR
    at, side = ring_position()
    kind = shared.dtype
    quarters, depth, width = shared.shape
    rows = depth // (ring * PAIR)
    split = (ring, PAIR, rows, width)
    shared_sum = lax.psum_scatter(shared, "batch", scatter_dimension=0, tiled=False).reshape(split)
    rest_pairs = rest.reshape((-1,) + split)
    out_pairs = out.reshape((-1,) + split)
    rest_parts, out_parts = rest_pairs.shape[0], out_pairs.shape[0]
    steps = small_steps(small)
    next(steps)
    given = {}

    def out_for(offset, where):
        spot = pick(out_pairs, (at + offset) % ring, 1)
        return pick(spot, where, 1)

    def exchange(offsets, tie):
        theirs = jnp.concatenate([out_for(offset + tie, 1 - side) for offset in offsets])
        arrived = swap_bit(theirs, 1)
        for number, offset in enumerate(offsets):
            given[offset] = arrived[number * out_parts : (number + 1) * out_parts]

    def main_term(offset):
        pair = pick(rest_pairs, (at + offset) % ring, 1).reshape(-1, rows, width)
        extra = given[offset].astype(jnp.float32)
        own = (out_for(offset, side).astype(jnp.float32) + extra).astype(kind)
        return jnp.concatenate([pair, own])

    def prepare(hop, ready):
        tie = after(ready)
        if hop == 0:
            tie = tie + after(shared_sum)
        exchange([hop, ring - hop] if hop else [0], tie)
        steps.send(tie)

    late = []

    def note(hop, ready):
        if hop == 1:
            late.append(after(ready))

    exchange([ring // 2], 0)
    total = ring_scatter(main_term, (rest_parts * PAIR + out_parts) // 2, prepare)
    steps.send(after(total))
    rest_share = keep_side(
        total[: rest_parts * PAIR].reshape(rest_parts, PAIR, rows, width), kind
    )
    shared_total = ring_scatter(
        lambda offset: pick(shared_sum, (at + offset) % ring), 1, note
    )
    share = jnp.concatenate([rest_share, total[rest_parts * PAIR :]])
    small_total = scale * steps.send(late[0])
    share = sum_batch((share + late[0].astype(jnp.float32)).astype(kind))
    shared_share = keep_side(shared_total[None], kind)[0].astype(kind)
    in_parts = [part.astype(jnp.float32) for part in batch_order(batch_copies(shared_share))]
    grad_in = jnp.concatenate(in_parts + [share[part] for part in range(rest_parts)], axis=1)
    grad_out = jnp.concatenate([share[rest_parts + part] for part in range(out_parts)], axis=1)
    return scale * grad_in, scale * grad_out, small_total


def layer_stats(values):
    mean_value = jnp.mean(values, axis=-1, keepdims=True)
    centred = values - mean_value
    inv_scale = lax.rsqrt(jnp.mean(centred * centred, axis=-1, keepdims=True) + epsilon)
    return centred * inv_scale, inv_scale


def norm_grad(upstream, normed, inv_scale):
    return (
        upstream
        - jnp.mean(upstream, axis=-1, keepdims=True)
        - normed * jnp.mean(upstream * normed, axis=-1, keepdims=True)
    ) * inv_scale


def rows_by(left, right):
    return jnp.dot(left, right, preferred_element_type=jnp.float32)


def rows_back(left, right):
    return lax.dot_general(
        left, right, (((1,), (1,)), ((), ())), preferred_element_type=jnp.float32
    )


def write_shifts(shifts, padded):
    span = shifts.shape[1]

    def shift(lanes):
        for by in range(SUBLANES):
            shifts[by, :, lanes] = padded[pl.ds(by, span), lanes]

    each_lane_block(padded.shape[1], shift)


def clear_margins(padded, length):
    zeros = jnp.zeros((MARGIN, padded.shape[1]), jnp.float32)
    padded[pl.ds(0, MARGIN), :] = zeros
    padded[pl.ds(MARGIN + length, MARGIN), :] = zeros


def each_block(width, size, body):
    def step(block, carry):
        body(block, pl.ds(pl.multiple_of(block * size, size), size))
        return carry

    lax.fori_loop(0, width // size, step, 0)


def each_lane_block(width, body):
    each_block(width, LANES, lambda block, lanes: body(lanes))


def shifted(shifts, offset, length, lanes):
    start = offset // SUBLANES * SUBLANES
    return shifts[offset % SUBLANES, pl.ds(start, length), lanes]


def part_copy(source, index, target, part, sems, base):
    return pltpu.make_async_copy(source.at[index], target.at[part], sems.at[base + part])


def start_parts(shared, rest, target, sems, base):
    for part in range(shared.shape[0]):
        part_copy(shared, part, target, part, sems, base).start()
    for part in range(rest.shape[0]):
        part_copy(rest, part, target, shared.shape[0] + part, sems, base).start()


def forward_kernel(
    info, incoming, frames, w_shared, w_rest, w_out, params, *refs, taps, length, width, aliased
):
    refs = refs[aliased:]
    outgoing, x_all, proj_all, swish_all, value_all, gate_all, mid_all, inv_all = refs[:8]
    (
        x_v, w_in_v, w_out_v, params_v, proj_v, swish_v, value_v, gate_v, mid_v, inv_v,
        padded, shifts, conv_v, out_v, in_sems, out_sems,
    ) = refs[8:]
    slot, active, first, valid = info[0], info[1], info[2], info[3]
    parts = w_in_v.shape[0]
    half = taps // 2

    @pl.when(active == 1)
    def run():
        x_copy = pltpu.make_async_copy(incoming, x_v, in_sems.at[0])
        frame_copy = pltpu.make_async_copy(frames.at[slot], x_v, in_sems.at[0])

        @pl.when(first == 1)
        def from_frames():
            frame_copy.start()

        @pl.when(first == 0)
        def from_neighbour():
            x_copy.start()

        params_copy = pltpu.make_async_copy(params, params_v, in_sems.at[1])
        params_copy.start()
        start_parts(w_shared, w_rest, w_in_v, in_sems, 2)
        w_out_copy = pltpu.make_async_copy(w_out, w_out_v, in_sems.at[2 + parts])
        w_out_copy.start()
        saves = []

        def save(source, target):
            copy = pltpu.make_async_copy(source, target, out_sems.at[len(saves)])
            copy.start()
            saves.append(copy)

        clear_margins(padded, length)
        x_copy.wait()
        params_copy.wait()
        source = x_v[...].astype(jnp.float32)
        save(x_v, x_all.at[slot])
        normed_in, unused = layer_stats(source)
        proj_v[...] = (normed_in * params_v[pl.ds(GAIN_A, 1), :]).astype(jnp.bfloat16)
        save(proj_v, proj_all.at[slot])
        part_width = w_in_v.shape[2]

        def into_value(part, lanes):
            part_copy(w_shared, 0, w_in_v, part, in_sems, 2).wait()
            value_v[:, lanes] = rows_by(proj_v[...], w_in_v[part])

        def into_gate(block, lanes):
            part = block + parts // 2
            part_copy(w_shared, 0, w_in_v, part, in_sems, 2).wait()
            gate_v[:, lanes] = jax.nn.sigmoid(rows_by(proj_v[...], w_in_v[part]))

        each_block(width, part_width, into_value)
        each_block(width, part_width, into_gate)
        save(value_v, value_all.at[slot])
        save(gate_v, gate_all.at[slot])
        rows = lax.broadcasted_iota(jnp.int32, (length, width), 0)
        mask = (rows < valid).astype(jnp.float32)
        padded[pl.ds(MARGIN, length), :] = value_v[...] * gate_v[...] * mask
        write_shifts(shifts, padded)

        def convolve(lanes):
            total = jnp.zeros((length, LANES), jnp.float32)
            for tap in range(taps):
                weight = params_v[pl.ds(tap, 1), lanes]
                total = total + shifted(shifts, tap + MARGIN - half, length, lanes) * weight
            conv_v[:, lanes] = total

        each_lane_block(width, convolve)
        normed_mid, inv_mid = layer_stats(conv_v[...])
        mid_v[...] = normed_mid
        inv_v[...] = jnp.broadcast_to(inv_mid, inv_v.shape)
        save(mid_v, mid_all.at[slot])
        save(inv_v, inv_all.at[slot])
        scaled_mid = normed_mid * params_v[pl.ds(GAIN_B, 1), :]
        swish_v[...] = (scaled_mid * jax.nn.sigmoid(scaled_mid)).astype(jnp.bfloat16)
        save(swish_v, swish_all.at[slot])
        w_out_copy.wait()

        def into_out(block, lanes):
            source = x_v[:, lanes].astype(jnp.float32)
            out_v[:, lanes] = (source + rows_by(swish_v[...], w_out_v[block])).astype(jnp.bfloat16)

        each_block(width, part_width, into_out)
        save(out_v, outgoing)
        for copy in saves:
            copy.wait()


def backward_kernel(
    info, incoming, cotangent, w_shared, w_rest, w_out, params,
    x_all, value_all, gate_all, mid_all, inv_all, *refs, taps, length, width, aliased
):
    refs = refs[aliased:]
    outgoing, input_all, grad_all, up_all, small_all, conv_all = refs[:6]
    (
        u_v, w_in_v, w_out_v, params_v, x_v, value_v, gate_v, mid_v, inv_v,
        padded_grad, shifts_grad, conv_v, grad_v, small_v, out_v,
        in_sems, out_sems,
    ) = refs[6:]
    slot, active, first, valid = info[0], info[1], info[2], info[3]
    parts = w_in_v.shape[0]
    half = taps // 2

    @pl.when(active == 1)
    def run():
        u_copy = pltpu.make_async_copy(incoming, u_v, in_sems.at[0])
        given_copy = pltpu.make_async_copy(cotangent.at[slot], u_v, in_sems.at[0])

        @pl.when(first == 1)
        def from_cotangent():
            given_copy.start()

        @pl.when(first == 0)
        def from_neighbour():
            u_copy.start()

        w_out_copy = pltpu.make_async_copy(w_out, w_out_v, in_sems.at[1])
        w_out_copy.start()
        loads = []
        for number, (source, target) in enumerate((
            (params, params_v),
            (value_all.at[slot], value_v),
            (gate_all.at[slot], gate_v),
            (mid_all.at[slot], mid_v),
            (inv_all.at[slot], inv_v),
            (x_all.at[slot], x_v),
        )):
            copy = pltpu.make_async_copy(source, target, in_sems.at[2 + number])
            copy.start()
            loads.append(copy)
        start_parts(w_shared, w_rest, w_in_v, in_sems, 8)
        saves = []

        def save(source, target):
            copy = pltpu.make_async_copy(source, target, out_sems.at[len(saves)])
            copy.start()
            saves.append(copy)

        clear_margins(padded_grad, length)
        small_v[...] = jnp.zeros_like(small_v)
        for copy in loads:
            copy.wait()
        rows = lax.broadcasted_iota(jnp.int32, (length, width), 0)
        mask = (rows < valid).astype(jnp.float32)
        u_copy.wait()
        save(u_v, up_all.at[slot])
        w_out_copy.wait()
        part_width = w_in_v.shape[2]
        conv_v[...] = jnp.zeros_like(conv_v)

        def into_swish(block, lanes):
            conv_v[...] += rows_back(u_v[:, lanes], w_out_v[block])

        each_block(width, part_width, into_swish)
        swish_grad = conv_v[...]
        normed_mid = mid_v[...]
        gain_b = params_v[pl.ds(GAIN_B, 1), :]
        scaled_mid = normed_mid * gain_b
        sigmoid_mid = jax.nn.sigmoid(scaled_mid)
        scaled_grad = swish_grad * (
            sigmoid_mid + scaled_mid * sigmoid_mid * (1.0 - sigmoid_mid)
        )
        small_v[pl.ds(SMALL_B, 1), :] = jnp.sum(scaled_grad * normed_mid, axis=0, keepdims=True)
        conv_grad = norm_grad(scaled_grad * gain_b, normed_mid, inv_v[:, :1])
        padded_grad[pl.ds(MARGIN, length), :] = conv_grad
        save(padded_grad.at[pl.ds(MARGIN, length), :], conv_all.at[slot])
        write_shifts(shifts_grad, padded_grad)

        def convolve(lanes):
            total = jnp.zeros((length, LANES), jnp.float32)
            for tap in range(taps):
                weight = params_v[pl.ds(tap, 1), lanes]
                total = total + shifted(shifts_grad, MARGIN + half - tap, length, lanes) * weight
            conv_v[:, lanes] = total

        each_lane_block(width, convolve)

        gated_grad = conv_v[...] * mask
        glu_gate = gate_v[...]
        grad_v[:, :width] = (gated_grad * glu_gate).astype(jnp.bfloat16)
        grad_v[:, width:] = (
            gated_grad * value_v[...] * glu_gate * (1.0 - glu_gate)
        ).astype(jnp.bfloat16)
        save(grad_v, grad_all.at[slot])
        conv_v[...] = jnp.zeros_like(conv_v)

        def into_input(part, lanes):
            part_copy(w_shared, 0, w_in_v, part, in_sems, 8).wait()
            conv_v[...] += rows_back(grad_v[:, lanes], w_in_v[part])

        each_block(2 * width, part_width, into_input)
        input_side = conv_v[...]
        normed_in, inv_in = layer_stats(x_v[...].astype(jnp.float32))
        small_v[pl.ds(SMALL_A, 1), :] = jnp.sum(input_side * normed_in, axis=0, keepdims=True)
        save(small_v, small_all.at[slot])
        gain_a = params_v[pl.ds(GAIN_A, 1), :]
        out_v[...] = (
            u_v[...].astype(jnp.float32) + norm_grad(input_side * gain_a, normed_in, inv_in)
        ).astype(jnp.bfloat16)
        save(out_v, outgoing)
        save(out_v, input_all.at[slot])
        for copy in saves:
            copy.wait()


def taps_kernel(valid, grads, values, gates, out, padded, shifts, *, taps, length, width):
    micro = pl.program_id(0)

    @pl.when(micro == 0)
    def clear():
        out[...] = jnp.zeros_like(out)
        clear_margins(padded, length)

    rows = lax.broadcasted_iota(jnp.int32, (length, width), 0)
    mask = (rows < valid[micro]).astype(jnp.float32)
    padded[pl.ds(MARGIN, length), :] = values[0] * gates[0] * mask
    write_shifts(shifts, padded)

    def correlate(lanes):
        given = grads[0, :, lanes]
        for tap in range(taps):
            product = given * shifted(shifts, tap + MARGIN - taps // 2, length, lanes)
            out[pl.ds(tap, 1), lanes] += jnp.sum(product, axis=0, keepdims=True)

    each_lane_block(width, correlate)


def taps_sums(valid, grads, values, gates, taps):
    micro, length, width = grads.shape
    span = length + 2 * MARGIN
    block = pl.BlockSpec((1, length, width), lambda index, valid: (index, 0, 0))
    return pl.pallas_call(
        functools.partial(taps_kernel, taps=taps, length=length, width=width),
        grid_spec=pltpu.PrefetchScalarGridSpec(
            num_scalar_prefetch=1,
            grid=(micro,),
            in_specs=[block] * 3,
            out_specs=pl.BlockSpec((GAIN_A, width), lambda index, valid: (0, 0)),
            scratch_shapes=[
                pltpu.VMEM((span, width), jnp.float32),
                pltpu.VMEM((SUBLANES, span - SUBLANES, width), jnp.float32),
            ],
        ),
        out_shape=jax.ShapeDtypeStruct((GAIN_A, width), jnp.float32),
        compiler_params=pltpu.CompilerParams(vmem_limit_bytes=32 * 1024 * 1024),
        cost_estimate=pl.CostEstimate(
            flops=2 * taps * micro * length * width,
            transcendentals=0,
            bytes_accessed=12 * micro * length * width,
        ),
    )(valid, grads, values, gates)


def stage_call(kernel, scratch, info, inputs, out_shapes, buffers, taps, length, width, cost, sems):
    anywhere = pl.BlockSpec(memory_space=pl.ANY)
    aliases = {}
    operands = list(inputs)
    aliased = 0
    if buffers is not None:
        aliased = len(buffers)
        aliases = {1 + len(inputs) + number: 1 + number for number in range(aliased)}
        operands += list(buffers)
    in_sems, out_sems = sems
    return pl.pallas_call(
        functools.partial(kernel, taps=taps, length=length, width=width, aliased=aliased),
        grid_spec=pltpu.PrefetchScalarGridSpec(
            num_scalar_prefetch=1,
            grid=(),
            in_specs=[anywhere] * len(operands),
            out_specs=[anywhere] * len(out_shapes),
            scratch_shapes=list(scratch)
            + [pltpu.SemaphoreType.DMA((in_sems,)), pltpu.SemaphoreType.DMA((out_sems,))],
        ),
        out_shape=out_shapes,
        input_output_aliases=aliases,
        compiler_params=pltpu.CompilerParams(vmem_limit_bytes=VMEM_LIMIT),
        cost_estimate=cost,
    )(info, *operands)


def stage_cost(length, width):
    return pl.CostEstimate(
        flops=6 * length * width * width,
        transcendentals=2 * length * width,
        bytes_accessed=6 * width * width,
    )


def forward_stage(info, incoming, frames, weights, params, buffers, taps):
    micro, length, width = frames.shape
    f32, bf16 = jnp.float32, jnp.bfloat16
    shape = jax.ShapeDtypeStruct
    outs = [shape((length, width), bf16)] + [
        shape((micro, length, width), dtype) for dtype in (bf16, bf16, bf16, f32, f32, f32)
    ] + [shape((micro, length, LANES), f32)]
    rows = functools.partial(pltpu.VMEM, (length, width))
    span = length + 2 * MARGIN
    scratch = [
        rows(bf16), pltpu.VMEM((IN_PARTS,) + weights[2].shape[1:], bf16), pltpu.VMEM(weights[2].shape, bf16),
        pltpu.VMEM(params.shape, f32), rows(bf16), rows(bf16), rows(f32), rows(f32), rows(f32),
        pltpu.VMEM((length, LANES), f32), pltpu.VMEM((span, width), f32),
        pltpu.VMEM((SUBLANES, span - SUBLANES, width), f32), rows(f32), rows(bf16),
    ]
    return stage_call(
        forward_kernel, scratch, info, (incoming, frames, *weights, params), outs, buffers,
        taps, length, width, stage_cost(length, width), (3 + IN_PARTS, 8),
    )


def backward_stage(info, incoming, cotangent, weights, params, saved, buffers, taps):
    micro, length, width = cotangent.shape
    f32, bf16 = jnp.float32, jnp.bfloat16
    shape = jax.ShapeDtypeStruct
    outs = [
        shape((length, width), bf16), shape((micro, length, width), bf16),
        shape((micro, length, 2 * width), bf16), shape((micro, length, width), bf16),
        shape((micro, 2 * SUBLANES, width), f32), shape((micro, length, width), f32),
    ]
    rows = functools.partial(pltpu.VMEM, (length, width))
    span = length + 2 * MARGIN
    lifted = pltpu.VMEM((SUBLANES, span - SUBLANES, width), f32)
    scratch = [
        rows(bf16), pltpu.VMEM((IN_PARTS,) + weights[2].shape[1:], bf16), pltpu.VMEM(weights[2].shape, bf16),
        pltpu.VMEM(params.shape, f32), rows(bf16), rows(f32), rows(f32), rows(f32),
        pltpu.VMEM((length, LANES), f32), pltpu.VMEM((span, width), f32), lifted, rows(f32),
        pltpu.VMEM((length, 2 * width), bf16), pltpu.VMEM((2 * SUBLANES, width), f32),
        rows(bf16),
    ]
    return stage_call(
        backward_kernel, scratch, info, (incoming, cotangent, *weights, params) + tuple(saved),
        outs, buffers, taps, length, width, stage_cost(length, width), (8 + IN_PARTS, 6),
    )


def send_active(x, senders, by):
    pairs = [(s, s + by) for s in senders if 0 <= s + by < lax.axis_size("section")]
    return lax.ppermute(x, "section", pairs)


def local(frames, cotangent, lengths, w_in, w_out, gain_pre, gain_mid, w_depth):
    sections = lax.axis_size("section")
    section_index = lax.axis_index("section")
    micro_count = frames.shape[0]
    frames_len = frames.shape[2]
    model_width = frames.shape[3]
    slots = micro_count + SKEW * (sections - 1)
    scale = 1.0 / math.sqrt(
        micro_count * frames_len * lax.axis_size("fsdp") * lax.axis_size("batch")
    )
    weights = gather_weights(w_in[0], w_out[0])
    taps = w_depth.shape[1]
    params = jnp.concatenate(
        [
            w_depth[0],
            jnp.zeros((GAIN_A - taps, model_width), jnp.float32),
            gain_pre,
            jnp.zeros((GAIN_B - GAIN_A - 1, model_width), jnp.float32),
            gain_mid,
            jnp.zeros((PARAM_ROWS - GAIN_B - 1, model_width), jnp.float32),
        ],
        axis=0,
    )
    frame_rows = frames.reshape(micro_count, frames_len, model_width)
    cotangent_rows = cotangent.reshape(micro_count, frames_len, model_width)

    def info_table(place):
        micro_index = jnp.arange(slots, dtype=jnp.int32) - SKEW * place
        active = (micro_index >= 0) & (micro_index < micro_count)
        slot = jnp.clip(micro_index, 0, micro_count - 1)
        first = jnp.broadcast_to(place == 0, active.shape)
        valid = jnp.take(lengths[:, 0], slot)
        return jnp.stack([slot, active.astype(jnp.int32), first.astype(jnp.int32), valid], axis=1)

    def active_at(slot, flipped):
        places = [p for p in range(sections) if 0 <= slot - SKEW * p < micro_count]
        return [sections - 1 - p for p in places] if flipped else places

    blank = jnp.zeros((frames_len, model_width), jnp.bfloat16)
    pending = [blank] * SKEW
    table = info_table(section_index)
    saved = None
    for slot in range(slots):
        outgoing, *saved = forward_stage(
            table[slot], pending.pop(0), frame_rows, weights, params, saved, taps
        )
        pending.append(send_active(outgoing, active_at(slot, False), 1))
    x_all, proj_all, swish_all, value_all, gate_all, mid_all, inv_all = saved
    kept = (x_all, value_all, gate_all, mid_all, inv_all)
    pending = [blank] * SKEW
    table = info_table(sections - 1 - section_index)
    grads = None
    for slot in range(slots):
        outgoing, *grads = backward_stage(
            table[slot], pending.pop(0), cotangent_rows, weights, params, kept,
            grads, taps,
        )
        pending.append(send_active(outgoing, active_at(slot, True), -1))
    input_all, grad_all, up_all, small_all, conv_all = grads
    total_rows = micro_count * frames_len
    width = weights[2].shape[2]
    quarters = weights[0].shape[0]
    proj_rows = proj_all.reshape(total_rows, model_width)
    grad_rows = grad_all.reshape(total_rows, 2 * model_width)
    swish_rows = swish_all.reshape(total_rows, model_width)
    upstream_rows = up_all.reshape(total_rows, model_width)

    def term(left, right):
        return lax.dot_general(
            left, right, (((0,), (0,)), ((), ())), preferred_element_type=jnp.float32
        ).astype(jnp.bfloat16)

    def terms(left, right, parts):
        return jnp.stack(
            [term(left, right[:, part * width : (part + 1) * width]) for part in parts]
        )

    shared_terms = terms(proj_rows, grad_rows, range(quarters))
    rest_terms = terms(proj_rows, grad_rows, range(quarters, IN_PARTS))
    out_terms = terms(swish_rows, upstream_rows, range(weights[2].shape[0]))
    small_rows = jnp.sum(small_all, axis=0)
    tap_rows = taps_sums(lengths[:, 0], conv_all, value_all, gate_all, taps)
    small = jnp.concatenate(
        [
            small_rows[SMALL_A : SMALL_A + 1],
            small_rows[SMALL_B : SMALL_B + 1],
            tap_rows[:taps],
        ],
        axis=0,
    )
    grad_in, grad_out, small_total = reduce_weights(
        shared_terms, rest_terms, out_terms, small, scale
    )
    input_grads = input_all.reshape(1, micro_count, 1, frames_len, model_width)
    return (
        input_grads,
        grad_in[None],
        grad_out[None],
        small_total[0:1],
        small_total[1:2],
        small_total[2:][None],
    )


def solution(mesh):
    in_specs = (
        P(None, ("fsdp", "batch"), None, None),
        P(None, ("fsdp", "batch"), None, None),
        P(None, ("fsdp", "batch")),
        P("section", "fsdp", None),
        P("section", "fsdp", None),
        P("section", None),
        P("section", None),
        P("section", None, None),
    )
    out_specs = (
        P("section", None, ("fsdp", "batch"), None, None),
        P("section", "fsdp", None),
        P("section", "fsdp", None),
        P("section", None),
        P("section", None),
        P("section", None, None),
    )
    return jax.shard_map(local, mesh=mesh, in_specs=in_specs, out_specs=out_specs, check_vma=False)
```
